1024 devices in a mesh: lat: 4 (over y_hi), lon: 256 (over y_lo, x, z, core).
Axes of the slice: x: 8, y: 8 (y_hi: 4, y_lo: 2; y = y_hi * 2 + y_lo), z: 8, core: 2. Of those that a mesh axis runs over, the one named last changes fastest.
Arguments:
- fields: bfloat16 [64, 4096, 128], P('lat', 'lon'), may hold values from -6 to 6
- weight_one: bfloat16 [7, 128, 128], replicated, may hold values from -0.1875 to 0.1875
- weight_two: bfloat16 [7, 128, 128], replicated, may hold values from -0.1875 to 0.1875
- basis_raw: bfloat16 [7, 64, 3, 9], replicated, may hold values from -1.5 to 1.5
- widths: int32 [64], replicated, may hold values from 1 to 4, as said below
- cotangent: bfloat16 [64, 4096, 128], P('lat', 'lon'), may hold values from -6 to 6
Outputs:
- output: bfloat16 [64, 4096, 128], P('lat', 'lon')
- dfields: bfloat16 [64, 4096, 128], P('lat', 'lon')
- grad_one: float32 [7, 128, 128], replicated
- grad_two: float32 [7, 128, 128], replicated
The draws below stay inside these ranges and needn't reach their ends.
Inputs may be any that keep to these rules, and one draw needn't show every extreme that they name: widths is 4 on the first and the last row of the grid.
All inputs are finite; a program needn't handle non-finite values.
Results may differ from the reference program's by a relative error of at most 0.0076.
Values may be sent and summed in bfloat16 or wider, within the bound.
A program may use at most 32 MiB of HBM per device.

```python
import math
import jax
import jax.numpy as jnp
from jax import lax

C = 128
K = 7
H = 4
NLAT = 64
NLON = 4096


def draw_widths(key, part):
    lat_rows = jnp.arange(NLAT, dtype=jnp.int32)
    drawn = jax.random.randint(key, (NLAT,), 1, H + 1, dtype=jnp.int32)
    edge = (lat_rows == 0) | (lat_rows == NLAT - 1)
    middle = lat_rows == NLAT // 2
    return jnp.where(edge, H, jnp.where(middle, 1, drawn)).astype(jnp.int32)


def shard_levels(stream_key, shape, split, least, top_value):
    loudness = 1.0
    for position, blocks in split:
        heights = jax.random.uniform(jax.random.fold_in(jax.random.fold_in(stream_key, 6), position), (blocks,), jnp.float32, least / len(split), top_value / len(split))
        loudness = loudness * jnp.repeat(jnp.exp(heights), shape[position] // blocks).reshape((-1,) + (1,) * (len(shape) - 1 - position))
    return loudness


def gaussian(rng, shape, scale, reach, cuts=(), held_as=jnp.bfloat16):
    result = jax.random.normal(rng, shape, jnp.float32) * scale
    if len(cuts) > 0:
        result = shard_levels(rng, shape, cuts, -0.22, 0.18) * result
    return jnp.clip(result, min=-reach, max=reach).astype(held_as)


def setup_inputs(seed: int = 0) -> dict:
    key_of = jax.random.split(jax.random.key(seed), 7)
    return {
        "fields": gaussian(key_of[0], (NLAT, NLON, C), 1.0, 6.0, ((0, 4), (1, 256))),
        "weight_one": gaussian(key_of[1], (K, C, C), (K * C) ** -0.5, 0.1875),
        "weight_two": gaussian(key_of[2], (K, C, C), (K * C) ** -0.5, 0.1875),
        "basis_raw": gaussian(key_of[3], (K, NLAT, 3, 2 * H + 1), (3 * (H + 1)) ** -0.5, 1.5),
        "widths": draw_widths(jax.random.fold_in(key_of[6], 71), 0),
        "cotangent": gaussian(key_of[5], (NLAT, NLON, C), 1.0, 6.0, ((0, 4), (1, 256))),
    }


def gelu_back(pre, upstream):
    return jax.vjp(jax.nn.gelu, pre)[1](upstream)[0]

def padded_basis(basis_raw, widths):
    offsets = jnp.abs(jnp.arange(2 * H + 1, dtype=jnp.int32) - H)
    inside = (offsets[None, :] <= widths[:, None]).astype(jnp.float32)
    masked = basis_raw.astype(jnp.float32) * inside[None, :, None, :]
    top_rows = masked[:, 0:1, ::-1, :]
    bottom = masked[:, NLAT - 1:NLAT, ::-1, :]
    zero_row = jnp.zeros_like(top_rows)
    return jnp.concatenate([zero_row, top_rows, masked, bottom, zero_row], axis=1)

def mirror_rows(field):
    top_rows = jnp.roll(field[0:1], NLON // 2, axis=1)
    bottom = jnp.roll(field[NLAT - 1:NLAT], NLON // 2, axis=1)
    return jnp.concatenate([top_rows, field, bottom], axis=0)

def row_forward(extended, weight, basis, row_index):
    lat_rows = lax.dynamic_slice_in_dim(extended, row_index, 3, 0).astype(jnp.float32)
    weights_row = lax.dynamic_index_in_dim(basis, row_index + 2, 1, keepdims=False)
    shifted = jnp.stack([jnp.roll(lat_rows, -(offset - H), axis=1) for offset in range(2 * H + 1)], axis=1)
    flattened = shifted.reshape(3 * (2 * H + 1), NLON * C)
    spread_row = jnp.dot(weights_row.reshape(K, 3 * (2 * H + 1)), flattened, precision=lax.Precision.HIGHEST)
    u_row = spread_row.reshape(K, NLON, C).transpose(1, 0, 2).astype(jnp.bfloat16)
    pre = jnp.dot(u_row.reshape(NLON, K * C), weight.reshape(K * C, C), preferred_element_type=jnp.float32)
    return (u_row, pre)

def block_forward(field, weight, basis):
    extended = mirror_rows(field)

    def one_row(row_index):
        u_row, pre = row_forward(extended, weight, basis, row_index)
        return (field[row_index].astype(jnp.float32) + jax.nn.gelu(pre)).astype(jnp.bfloat16)
    return lax.map(one_row, jnp.arange(NLAT, dtype=jnp.int32))

def block_grads(field, weight, basis, upstream):
    extended = mirror_rows(field)

    def step_row(summed, row_index):
        u_row, pre = row_forward(extended, weight, basis, row_index)
        dconv = gelu_back(pre, upstream[row_index].astype(jnp.float32)).astype(jnp.bfloat16)
        summed = summed + jnp.dot(u_row.reshape(NLON, K * C).T, dconv, preferred_element_type=jnp.float32)
        return (summed, dconv)
    summed, dconv = lax.scan(step_row, jnp.zeros((K * C, C), jnp.float32), jnp.arange(NLAT, dtype=jnp.int32))
    return (dconv, summed.reshape(K, C, C))

def block_input_grad(dconv, weight, basis, upstream):
    extended = mirror_rows(dconv)
    weight_back = weight.reshape(K * C, C).T

    def one_row(row_index):
        lat_rows = lax.dynamic_slice_in_dim(extended, row_index, 3, 0)
        mixed = jnp.dot(lat_rows.reshape(3 * NLON, C), weight_back, preferred_element_type=jnp.float32)
        mixed = lax.optimization_barrier(mixed.astype(jnp.bfloat16)).astype(jnp.float32).reshape(3, NLON, K, C)
        summed = upstream[row_index].astype(jnp.float32)
        for row_tap in range(3):
            weights_row = lax.dynamic_index_in_dim(basis, row_index + 3 - row_tap, 1, keepdims=False)[:, row_tap, :]
            partial_rows = jnp.einsum('kt,lkc->tlc', weights_row, mixed[2 - row_tap], precision=lax.Precision.HIGHEST)
            for offset in range(2 * H + 1):
                summed = summed + jnp.roll(partial_rows[offset], offset - H, axis=0)
        return summed
    return lax.map(one_row, jnp.arange(NLAT, dtype=jnp.int32))

def reference(fields, weight_one, weight_two, basis_raw, widths, cotangent):
    basis = padded_basis(basis_raw, widths)
    hidden = block_forward(fields, weight_one, basis)
    output = block_forward(hidden, weight_two, basis)
    dconv_two, grad_two = block_grads(hidden, weight_two, basis, cotangent)
    dhidden = block_input_grad(dconv_two, weight_two, basis, cotangent)
    dconv_one, grad_one = block_grads(fields, weight_one, basis, dhidden)
    dfields = block_input_grad(dconv_one, weight_one, basis, dhidden).astype(jnp.bfloat16)
    scale = 1.0 / math.sqrt(NLAT * NLON)
    return (output, dfields, grad_one * scale, grad_two * scale)
```

```python
import functools
import math

import jax
import jax.numpy as jnp
from jax import lax
from jax.experimental import pallas as pl
from jax.experimental.pallas import tpu as pltpu
from jax.sharding import PartitionSpec as P

MESH = pl.DeviceIdType.MESH
RING = 8


def shifted(block, axis, distance):
    devices = range(lax.axis_size(axis))
    route = [((i - distance) % len(devices), i) for i in devices]
    return lax.ppermute(block, axis, route)


def with_halo(block, sides, width, periodic):
    for axis, dim in sides:
        count = lax.axis_size(axis)
        forward = [(i, i + 1) for i in range(count - 1)]
        if periodic:
            forward.append((count - 1, 0))
        backward = [(target, source) for source, target in forward]
        low = lax.ppermute(
            lax.slice_in_dim(block, block.shape[dim] - width, None, axis=dim), axis, forward
        )
        high = lax.ppermute(lax.slice_in_dim(block, 0, width, axis=dim), axis, backward)
        block = jnp.concatenate([low, block, high], axis=dim)
    return block


def gelu_back(pre, upstream):
    return jax.vjp(jax.nn.gelu, pre)[1](upstream)[0]


def padded_basis(basis_raw, widths):
    tap_count = basis_raw.shape[3]
    reach = (tap_count - 1) // 2
    distance = jnp.abs(jnp.arange(tap_count, dtype=jnp.int32) - reach)
    inside = (distance[None, :] <= widths[:, None]).astype(jnp.bfloat16)
    masked = basis_raw * inside[None, :, None, :]
    top_rows = masked[:, 0:1, ::-1, :]
    bottom = masked[:, -1:, ::-1, :]
    zero_row = jnp.zeros_like(top_rows)
    return jnp.concatenate([zero_row, top_rows, masked, bottom, zero_row], axis=1)


def selector(out_len, in_len, tap_count, flipped):
    lon_out = jnp.arange(out_len, dtype=jnp.int32)[None, :, None]
    lon_in = jnp.arange(in_len, dtype=jnp.int32)[None, None, :]
    offset = jnp.arange(tap_count, dtype=jnp.int32)[:, None, None]
    target = lon_out + (tap_count - 1) - offset if flipped else lon_out + offset
    return (lon_in == target).astype(jnp.bfloat16)


def spread_local(extended, basis_rows):
    row_count = basis_rows.shape[1]
    tap_count = basis_rows.shape[3]
    in_len = extended.shape[1]
    out_len = in_len - (tap_count - 1)
    picker = selector(out_len, in_len, tap_count, False)
    summed = None
    for row_tap in range(3):
        band_rows = jnp.einsum(
            "kit,tlm->kilm",
            basis_rows[:, :, row_tap, :],
            picker,
            preferred_element_type=jnp.float32,
        ).astype(jnp.bfloat16)
        partial_rows = jnp.einsum(
            "kilm,imc->ilkc",
            band_rows,
            extended[row_tap : row_tap + row_count],
            preferred_element_type=jnp.float32,
        )
        summed = partial_rows if summed is None else summed + partial_rows
    return summed.astype(jnp.bfloat16)


def gather_back(extended, source_basis):
    row_count = extended.shape[0] - 2
    tap_count = source_basis.shape[3]
    in_len = extended.shape[1]
    out_len = in_len - (tap_count - 1)
    picker = selector(out_len, in_len, tap_count, True)
    summed = None
    for row_tap in range(3):
        first_tap = 2 - row_tap
        weights_rows = source_basis[:, first_tap : first_tap + row_count, row_tap, :]
        band_rows = jnp.einsum(
            "kjt,tlm->kjlm", weights_rows, picker, preferred_element_type=jnp.float32
        ).astype(jnp.bfloat16)
        partial_rows = jnp.einsum(
            "kjlm,jmkc->jlc",
            band_rows,
            extended[first_tap : first_tap + row_count],
            preferred_element_type=jnp.float32,
        )
        summed = partial_rows if summed is None else summed + partial_rows
    return summed


def mix_forward(spread_vals, weight):
    return jnp.einsum("ilkc,kco->ilo", spread_vals, weight, preferred_element_type=jnp.float32)


def mix_back(dconv, weight):
    return jnp.einsum("ilo,kco->ilkc", dconv, weight, preferred_element_type=jnp.float32).astype(
        jnp.bfloat16
    )


def weight_terms(spread_vals, dconv):
    return jnp.einsum("ilkc,ilo->kco", spread_vals, dconv, preferred_element_type=jnp.float32)


def mirror_fix(heightened, depth):
    row_count = heightened.shape[0] - 2 * depth
    top_rows = jnp.flip(heightened[depth : 2 * depth], 0)
    bottom = jnp.flip(heightened[row_count : row_count + depth], 0)
    mirrored = shifted(jnp.concatenate([top_rows, bottom], 0), "lon", lax.axis_size("lon") // 2)
    band_index = lax.axis_index("lat")
    new_top = jnp.where(band_index == 0, mirrored[:depth], heightened[:depth])
    new_bottom = jnp.where(
        band_index == lax.axis_size("lat") - 1, mirrored[depth:], heightened[row_count + depth :]
    )
    return jnp.concatenate([new_top, heightened[depth : row_count + depth], new_bottom], 0)


def extend_each(field, reach):
    widened = with_halo(field, (("lon", 1),), reach, True)
    heightened = with_halo(widened, (("lat", 0),), 1, False)
    return mirror_fix(heightened, 1)


def coordinates():
    lat = lax.axis_index("lat")
    lon = lax.axis_index("lon")
    core = lax.rem(lon, 2)
    z = lax.rem(lax.div(lon, 2), RING)
    x = lax.rem(lax.div(lon, 2 * RING), RING)
    y = lat * 2 + lax.div(lon, 2 * RING * RING)
    return core, x, y, z


def device_at(core, x, y, z):
    return (lax.div(y, 2), lax.rem(y, 2) * (2 * RING * RING) + x * (2 * RING) + z * 2 + core)


def ring_peer(here, stage, step):
    core, x, y, z = here
    other = 1 - core
    on_x, on_y, on_z = ((other, core, 0), (0, other, core), (core, 0, other))[stage]
    return device_at(
        core,
        lax.rem(x + step * on_x, RING),
        lax.rem(y + step * on_y, RING),
        lax.rem(z + step * on_z, RING),
    )


def ring_index(here, stage):
    core, x, y, z = here
    first, second = ((x, y), (y, z), (z, x))[stage]
    return first * (1 - core) + second * core


def partner_of(here):
    core, x, y, z = here
    return device_at(1 - core, x, y, z)


def greet_reducers(here, barrier):
    pl.semaphore_signal(barrier, inc=1, device_id=partner_of(here), device_id_type=MESH)
    for stage in range(3):

        def greet(step, carry, stage=stage):
            pl.semaphore_signal(
                barrier, inc=1, device_id=ring_peer(here, stage, step), device_id_type=MESH
            )
            return carry

        lax.fori_loop(1, RING, greet, 0)
    return 1 + 3 * (RING - 1)


def exchange(here, stage, source_of, landing, send_sem, recv_sem, arrived):
    def copy(step):
        return pltpu.make_async_remote_copy(
            src_ref=source_of(step),
            dst_ref=landing.at[step],
            send_sem=send_sem.at[step],
            recv_sem=recv_sem.at[step],
            device_id=ring_peer(here, stage, step),
            device_id_type=MESH,
        )

    def start(step, carry):
        copy(step).start()
        return carry

    def finish(step, carry):
        copy(step).wait_recv()
        arrived(step)
        return carry

    def drain(step, carry):
        copy(step).wait_send()
        return carry

    lax.fori_loop(1, RING, start, 0)
    lax.fori_loop(1, RING, finish, 0)
    lax.fori_loop(1, RING, drain, 0)


def reduce_everywhere(here, terms, out_ref, scale, scratch):
    (pair_out, pair_in, halves, wide_out, wide_in, narrow, narrow_out, narrow_in,
     last, spread_in, chunk, own_half, other_half, pair_send, pair_recv, sends, recvs) = scratch
    core = here[0]
    pair_out[...] = terms[1 - core].astype(jnp.bfloat16)
    swap = pltpu.make_async_remote_copy(
        src_ref=pair_out, dst_ref=pair_in, send_sem=pair_send.at[0], recv_sem=pair_recv.at[0],
        device_id=partner_of(here), device_id_type=MESH,
    )
    swap.start()
    narrow[...] = jnp.zeros(narrow.shape, narrow.dtype)
    swap.wait_recv()
    halves[...] = terms[core] + pair_in[...].astype(jnp.float32)
    wide_out[...] = halves[...].astype(jnp.bfloat16)

    at_a, at_b, at_c = (ring_index(here, stage) for stage in range(3))
    rows = halves.shape[1]
    tile = narrow.shape[1]
    own = narrow.at[: rows // tile]
    own[...] = halves[at_a].reshape(rows // tile, tile, -1)

    def add_wide(step):
        own[...] += wide_in[step].astype(jnp.float32).reshape(rows // tile, tile, -1)

    exchange(here, 0, lambda step: wide_out.at[lax.rem(at_a + step, RING)], wide_in,
             sends.at[0], recvs.at[0], add_wide)
    narrow_out[...] = narrow[...].astype(jnp.bfloat16)
    last[0] = narrow[at_b]

    def add_narrow(step):
        last[0] += narrow_in[step].astype(jnp.float32)

    exchange(here, 1, lambda step: narrow_out.at[lax.rem(at_b + step, RING)], narrow_in,
             sends.at[1], recvs.at[1], add_narrow)
    exchange(here, 2, lambda step: last.at[0], last, sends.at[2], recvs.at[2], lambda step: None)

    total = last[at_c]
    for source in range(1, RING):
        total = total + last[lax.rem(at_c - source + RING, RING)]
    spread_in[0] = (total * scale).astype(jnp.bfloat16)
    exchange(here, 1, lambda step: spread_in.at[0], spread_in, sends.at[3], recvs.at[3],
             lambda step: None)
    for source in range(rows // tile):
        chunk[0, source * tile : (source + 1) * tile] = spread_in[
            lax.rem(at_b - source + RING, RING)
        ]

    def across(step):
        return pltpu.make_async_remote_copy(
            src_ref=chunk.at[step], dst_ref=other_half.at[step],
            send_sem=pair_send.at[1 + step], recv_sem=pair_recv.at[1 + step],
            device_id=partner_of(here), device_id_type=MESH,
        )

    across(0).start()
    exchange(here, 0, lambda step: chunk.at[0], chunk, sends.at[4], recvs.at[4],
             lambda step: across(step).start())
    at_partner = at_a * 0 + here[2] * (1 - core) + here[1] * core

    def place(source, carry):
        out_ref[core, source] = chunk[lax.rem(at_a - source + RING, RING)]
        return carry

    lax.fori_loop(0, RING, place, 0)

    def settle(step, carry):
        across(step).wait()
        return carry

    lax.fori_loop(0, RING, settle, 0)

    def place_other(source, carry):
        out_ref[1 - core, source] = other_half[lax.rem(at_partner - source + RING, RING)]
        return carry

    lax.fori_loop(0, RING, place_other, 0)
    swap.wait_send()


def reduce_scratch(rows, lanes):
    tile = 16
    low, high = jnp.bfloat16, jnp.float32
    return [
        pltpu.VMEM((RING, rows, lanes), low),
        pltpu.VMEM((RING, rows, lanes), low),
        pltpu.VMEM((RING, rows, lanes), high),
        pltpu.VMEM((RING, rows, lanes), low),
        pltpu.VMEM((RING, rows, lanes), low),
        pltpu.VMEM((RING, tile, lanes), high),
        pltpu.VMEM((RING, tile, lanes), low),
        pltpu.VMEM((RING, tile, lanes), low),
        pltpu.VMEM((RING, tile, lanes), high),
        pltpu.VMEM((RING, tile, lanes), low),
        pltpu.VMEM((RING, rows, lanes), low),
        pltpu.VMEM((RING, rows, lanes), low),
        pltpu.VMEM((RING, rows, lanes), low),
        pltpu.SemaphoreType.DMA((1 + RING,)),
        pltpu.SemaphoreType.DMA((1 + RING,)),
        pltpu.SemaphoreType.DMA((5, RING)),
        pltpu.SemaphoreType.DMA((5, RING)),
    ]


def reduce_kernel(scale, terms_ref, out_ref, *scratch):
    here = coordinates()
    barrier = pltpu.get_barrier_semaphore()
    pl.semaphore_wait(barrier, greet_reducers(here, barrier))
    reduce_everywhere(here, terms_ref, out_ref, scale, scratch)


def reduced(grad_one, grad_two, scale):
    kernels, depth, lanes = grad_one.shape
    rows = kernels * depth // RING
    terms = jnp.stack([grad_one, grad_two]).reshape(2, RING, rows, lanes)
    summed = pl.pallas_call(
        functools.partial(reduce_kernel, scale),
        out_shape=jax.ShapeDtypeStruct(terms.shape, jnp.bfloat16),
        in_specs=[pl.BlockSpec(memory_space=pltpu.VMEM)],
        out_specs=pl.BlockSpec(memory_space=pltpu.VMEM),
        scratch_shapes=reduce_scratch(rows, lanes),
        compiler_params=pltpu.CompilerParams(collective_id=0, has_side_effects=True),
    )(terms)
    summed = summed.astype(jnp.float32).reshape(2, kernels, depth, lanes)
    return summed[0], summed[1]


def body(fields, weight_one, weight_two, basis_raw, widths, cotangent):
    lat_count = fields.shape[0]
    lon_count = fields.shape[1]
    reach = (basis_raw.shape[3] - 1) // 2
    basis = padded_basis(basis_raw, widths)
    first_row = lax.axis_index("lat") * lat_count

    def output_rows(row_count):
        return lax.dynamic_slice_in_dim(basis, first_row + 2, row_count, 1)

    def source_rows(row_count):
        return lax.dynamic_slice_in_dim(basis, first_row + 1, row_count + 2, 1)

    upstream = cotangent.astype(jnp.float32)
    ext_fields = extend_each(fields, reach)
    u_one = spread_local(ext_fields, output_rows(lat_count))
    pre_one = mix_forward(u_one, weight_one)
    hidden = (fields.astype(jnp.float32) + jax.nn.gelu(pre_one)).astype(jnp.bfloat16)
    ext_hidden = extend_each(hidden, reach)
    u_two = spread_local(ext_hidden, output_rows(lat_count))
    pre_two = mix_forward(u_two, weight_two)
    output = (hidden.astype(jnp.float32) + jax.nn.gelu(pre_two)).astype(jnp.bfloat16)
    dconv_two = gelu_back(pre_two, upstream).astype(jnp.bfloat16)
    grad_two = weight_terms(u_two, dconv_two)
    ext_two = extend_each(dconv_two, reach)
    du_two = mix_back(ext_two, weight_two)
    dhidden = upstream + gather_back(du_two, source_rows(lat_count))
    dconv_one = gelu_back(pre_one, dhidden).astype(jnp.bfloat16)
    ext_one = extend_each(dconv_one, reach)
    grad_one = weight_terms(u_one, dconv_one)
    du_one = mix_back(ext_one, weight_one)
    dfields = (dhidden + gather_back(du_one, source_rows(lat_count))).astype(jnp.bfloat16)
    scale = 1.0 / math.sqrt(lat_count * lax.axis_size("lat") * lon_count * lax.axis_size("lon"))
    return (output, dfields, *reduced(grad_one, grad_two, scale))


def solution(mesh):
    placed = (P("lat", "lon", None), P(), P(), P(), P(), P("lat", "lon", None))
    return jax.shard_map(
        body,
        mesh=mesh,
        in_specs=placed,
        out_specs=(P("lat", "lon", None), P("lat", "lon", None), P(), P()),
        check_vma=False,
    )
```

```python
import functools
import math

import jax
import jax.numpy as jnp
from jax import lax
from jax.experimental import pallas as pl
from jax.experimental.pallas import tpu as pltpu
from jax.sharding import PartitionSpec as P

MESH = pl.DeviceIdType.MESH
RING = 8
RIM = 8
LANES = 128
GELU_SLOPE = math.sqrt(2.0 / math.pi)
GELU_CUBIC = 0.044715


def padded_basis(basis_raw, widths):
    tap_count = basis_raw.shape[3]
    reach = (tap_count - 1) // 2
    distance = jnp.abs(jnp.arange(tap_count, dtype=jnp.int32) - reach)
    inside = (distance[None, :] <= widths[:, None]).astype(jnp.bfloat16)
    masked = basis_raw * inside[None, :, None, :]
    top_rows = masked[:, 0:1, ::-1, :]
    bottom = masked[:, -1:, ::-1, :]
    zero_row = jnp.zeros_like(top_rows)
    return jnp.concatenate([zero_row, top_rows, masked, bottom, zero_row], axis=1)


def coordinates():
    lat = lax.axis_index("lat")
    lon = lax.axis_index("lon")
    core = lax.rem(lon, 2)
    z = lax.rem(lax.div(lon, 2), RING)
    x = lax.rem(lax.div(lon, 2 * RING), RING)
    y = lat * 2 + lax.div(lon, 2 * RING * RING)
    return core, x, y, z


def device_at(core, x, y, z):
    return (lax.div(y, 2), lax.rem(y, 2) * (2 * RING * RING) + x * (2 * RING) + z * 2 + core)


def ring_peer(here, stage, step):
    core, x, y, z = here
    other = 1 - core
    on_x, on_y, on_z = ((other, core, 0), (0, other, core), (core, 0, other))[stage]
    return device_at(
        core,
        lax.rem(x + step * on_x, RING),
        lax.rem(y + step * on_y, RING),
        lax.rem(z + step * on_z, RING),
    )


def ring_index(here, stage):
    core, x, y, z = here
    first, second = ((x, y), (y, z), (z, x))[stage]
    return first * (1 - core) + second * core


def partner_of(here):
    core, x, y, z = here
    return device_at(1 - core, x, y, z)


def greet_reducers(here, barrier):
    pl.semaphore_signal(barrier, inc=1, device_id=partner_of(here), device_id_type=MESH)
    for stage in range(3):

        def greet(step, carry, stage=stage):
            pl.semaphore_signal(
                barrier, inc=1, device_id=ring_peer(here, stage, step), device_id_type=MESH
            )
            return carry

        lax.fori_loop(1, RING, greet, 0)
    return 1 + 3 * (RING - 1)


def exchange(here, stage, source_of, landing, send_sem, recv_sem, arrived, meanwhile=None):
    def copy(step):
        return pltpu.make_async_remote_copy(
            src_ref=source_of(step),
            dst_ref=landing.at[step],
            send_sem=send_sem.at[step],
            recv_sem=recv_sem.at[step],
            device_id=ring_peer(here, stage, step),
            device_id_type=MESH,
        )

    def start(step, carry):
        copy(step).start()
        return carry

    def finish(step, carry):
        copy(step).wait_recv()
        arrived(step)
        return carry

    def drain(step, carry):
        copy(step).wait_send()
        return carry

    lax.fori_loop(1, RING, start, 0)
    if meanwhile is not None:
        meanwhile()
    lax.fori_loop(1, RING, finish, 0)
    lax.fori_loop(1, RING, drain, 0)


def reduce_everywhere(here, terms, out_ref, scale, scratch, meanwhile):
    (pair_out, pair_in, halves, wide_out, wide_in, narrow, narrow_out, narrow_in,
     last, spread_in, chunk, own_half, other_half, pair_send, pair_recv, sends, recvs) = scratch
    core = here[0]
    pair_out[...] = terms[1 - core].astype(jnp.bfloat16)
    swap = pltpu.make_async_remote_copy(
        src_ref=pair_out, dst_ref=pair_in, send_sem=pair_send.at[0], recv_sem=pair_recv.at[0],
        device_id=partner_of(here), device_id_type=MESH,
    )
    swap.start()
    narrow[...] = jnp.zeros(narrow.shape, narrow.dtype)
    swap.wait_recv()
    halves[...] = terms[core] + pair_in[...].astype(jnp.float32)
    wide_out[...] = halves[...].astype(jnp.bfloat16)

    at_a, at_b, at_c = (ring_index(here, stage) for stage in range(3))
    rows = halves.shape[1]
    tile = narrow.shape[1]
    own = narrow.at[: rows // tile]
    own[...] = halves[at_a].reshape(rows // tile, tile, -1)

    def add_wide(step):
        own[...] += wide_in[step].astype(jnp.float32).reshape(rows // tile, tile, -1)

    exchange(here, 0, lambda step: wide_out.at[lax.rem(at_a + step, RING)], wide_in,
             sends.at[0], recvs.at[0], add_wide, meanwhile)
    narrow_out[...] = narrow[...].astype(jnp.bfloat16)
    last[0] = narrow[at_b]

    def add_narrow(step):
        last[0] += narrow_in[step].astype(jnp.float32)

    exchange(here, 1, lambda step: narrow_out.at[lax.rem(at_b + step, RING)], narrow_in,
             sends.at[1], recvs.at[1], add_narrow)
    exchange(here, 2, lambda step: last.at[0], last, sends.at[2], recvs.at[2], lambda step: None)

    total = last[at_c]
    for source in range(1, RING):
        total = total + last[lax.rem(at_c - source + RING, RING)]
    spread_in[0] = (total * scale).astype(jnp.bfloat16)
    exchange(here, 1, lambda step: spread_in.at[0], spread_in, sends.at[3], recvs.at[3],
             lambda step: None)
    for source in range(rows // tile):
        chunk[0, source * tile : (source + 1) * tile] = spread_in[
            lax.rem(at_b - source + RING, RING)
        ]

    def across(step):
        return pltpu.make_async_remote_copy(
            src_ref=chunk.at[step], dst_ref=other_half.at[step],
            send_sem=pair_send.at[1 + step], recv_sem=pair_recv.at[1 + step],
            device_id=partner_of(here), device_id_type=MESH,
        )

    across(0).start()
    exchange(here, 0, lambda step: chunk.at[0], chunk, sends.at[4], recvs.at[4],
             lambda step: across(step).start())
    at_partner = at_a * 0 + here[2] * (1 - core) + here[1] * core

    def place(source, carry):
        out_ref[core, source] = chunk[lax.rem(at_a - source + RING, RING)]
        return carry

    lax.fori_loop(0, RING, place, 0)

    def settle(step, carry):
        across(step).wait()
        return carry

    lax.fori_loop(0, RING, settle, 0)

    def place_other(source, carry):
        out_ref[1 - core, source] = other_half[lax.rem(at_partner - source + RING, RING)]
        return carry

    lax.fori_loop(0, RING, place_other, 0)
    swap.wait_send()


def reduce_scratch(rows, lanes):
    tile = 16
    low, high = jnp.bfloat16, jnp.float32
    return [
        pltpu.VMEM((RING, rows, lanes), low),
        pltpu.VMEM((RING, rows, lanes), low),
        pltpu.VMEM((RING, rows, lanes), high),
        pltpu.VMEM((RING, rows, lanes), low),
        pltpu.VMEM((RING, rows, lanes), low),
        pltpu.VMEM((RING, tile, lanes), high),
        pltpu.VMEM((RING, tile, lanes), low),
        pltpu.VMEM((RING, tile, lanes), low),
        pltpu.VMEM((RING, tile, lanes), high),
        pltpu.VMEM((RING, tile, lanes), low),
        pltpu.VMEM((RING, rows, lanes), low),
        pltpu.VMEM((RING, rows, lanes), low),
        pltpu.VMEM((RING, rows, lanes), low),
        pltpu.SemaphoreType.DMA((1 + RING,)),
        pltpu.SemaphoreType.DMA((1 + RING,)),
        pltpu.SemaphoreType.DMA((5, RING)),
        pltpu.SemaphoreType.DMA((5, RING)),
    ]


def gelu_parts(pre):
    square = pre * pre
    bent = jnp.tanh(GELU_SLOPE * pre * (1.0 + GELU_CUBIC * square))
    value = 0.5 * pre * (1.0 + bent)
    slope = 0.5 * (1.0 + bent) + 0.5 * pre * (1.0 - bent * bent) * GELU_SLOPE * (
        1.0 + 3.0 * GELU_CUBIC * square
    )
    return value, slope


def halo_devices():
    lat = lax.axis_index("lat")
    lon = lax.axis_index("lon")
    lats = lax.axis_size("lat")
    lons = lax.axis_size("lon")
    at_top = lax.div(lats - 1 - lat, lats - 1)
    at_bottom = lax.div(lat, lats - 1)
    right = lax.rem(lon + 1, lons)
    left = lax.rem(lon + lons - 1, lons)
    ends = []
    for at_end, step, row_slot in ((at_top, -1, 1 - at_top), (at_bottom, 1, at_bottom)):
        far_lat = lat + step * (1 - at_end)
        turn = at_end * (lons // 2)
        ends.append(
            (
                row_slot,
                (far_lat, lax.rem(lon + turn, lons)),
                (far_lat, lax.rem(right + turn, lons)),
                (far_lat, lax.rem(left + turn, lons)),
            )
        )
    return (lat, right), (lat, left), ends


def greet_halo(barrier):
    right, left, ends = halo_devices()
    others = [right, left]
    for _, straight, to_right, to_left in ends:
        others += [straight, to_right, to_left]
    for other in others:
        pl.semaphore_signal(barrier, inc=1, device_id=other, device_id_type=MESH)
    return len(others)


def halo_outgoing(stage, halo):
    own, first_cols, last_cols, west, east, row_in, send_sem, recv_sem = halo
    rows = own.shape[1]
    right, left, ends = halo_devices()
    count = 0

    def copy(source, target, slot, device):
        nonlocal count
        count += 1
        return pltpu.make_async_remote_copy(
            src_ref=source, dst_ref=target, send_sem=send_sem.at[stage, count - 1],
            recv_sem=recv_sem.at[stage, slot], device_id=device, device_id_type=MESH,
        )

    outgoing = []
    for (slot, straight, to_right, to_left), row in zip(ends, (0, rows - 1)):
        edge = slot * (rows + 1)
        outgoing += [
            copy(last_cols.at[stage, row], west.at[stage, edge], 4 + slot, to_right),
            copy(first_cols.at[stage, row], east.at[stage, edge], 6 + slot, to_left),
            copy(own.at[stage, row], row_in.at[stage, slot], 2 + slot, straight),
        ]
    inner = pl.ds(1, rows)
    outgoing += [
        copy(last_cols.at[stage], west.at[stage, inner], 0, right),
        copy(first_cols.at[stage], east.at[stage, inner], 1, left),
    ]
    return outgoing


def halo_incoming(stage, halo):
    own, first_cols, last_cols, west, east, row_in, send_sem, recv_sem = halo
    rows = own.shape[1]
    right, left, _ = halo_devices()

    def copy(source, target, slot, device):
        return pltpu.make_async_remote_copy(
            src_ref=source, dst_ref=target, send_sem=send_sem.at[stage, slot],
            recv_sem=recv_sem.at[stage, slot], device_id=device, device_id_type=MESH,
        )

    inner = pl.ds(1, rows)
    incoming = [
        copy(last_cols.at[stage], west.at[stage, inner], 0, right),
        copy(first_cols.at[stage], east.at[stage, inner], 1, left),
    ]
    for slot in range(2):
        edge = slot * (rows + 1)
        incoming += [
            copy(own.at[stage, 0], row_in.at[stage, slot], 2 + slot, right),
            copy(last_cols.at[stage, 0], west.at[stage, edge], 4 + slot, right),
            copy(first_cols.at[stage, 0], east.at[stage, edge], 6 + slot, right),
        ]
    return incoming


def halo_prepare(stage, field, halo):
    own, first_cols, last_cols = halo[:3]
    own[stage] = field.astype(own.dtype)
    first_cols[stage] = field[:, :RIM].astype(own.dtype)
    last_cols[stage] = field[:, -RIM:].astype(own.dtype)


def halo_send(stage, halo):
    for copy in halo_outgoing(stage, halo):
        copy.start()


def halo_receive(stage, halo, extended):
    own, _, _, west, east, row_in = halo[:6]
    rows, cols = own.shape[1], own.shape[2]
    period = cols + 2 * RIM

    for row in range(rows):
        start = (row + 1) * period + 2 * RIM
        extended[start : start + cols] = own[stage, row]
    for copy in halo_incoming(stage, halo):
        copy.wait_recv()
    for slot in range(2):
        start = slot * (rows + 1) * period + 2 * RIM
        extended[start : start + cols] = row_in[stage, slot]
    west_rim = west[stage].astype(jnp.float32)
    east_rim = east[stage].astype(jnp.float32)
    blank = jnp.zeros((1, RIM, LANES), jnp.float32)
    rims = jnp.concatenate(
        [
            jnp.concatenate([blank, east_rim], axis=0),
            jnp.concatenate([west_rim, blank], axis=0),
        ],
        axis=1,
    ).astype(own.dtype)
    for row in range(rows + 3):
        extended[row * period : row * period + 2 * RIM] = rims[row]


def apply_bands(bands, extended, spread):
    rows, height = bands.shape[0], bands.shape[1]
    kernels = spread.shape[1] // LANES
    cols = spread.shape[0] // rows
    period = cols + 2 * RIM
    group = 4

    def some_rows(index, carry):
        for part in range(group):
            row = index * group + part
            window = extended[pl.ds(pl.multiple_of(row * period, period), LANES)]
            made = jnp.dot(
                bands[row], window, preferred_element_type=jnp.float32
            ).astype(spread.dtype)
            for kernel in range(kernels):
                spread[
                    pl.ds(pl.multiple_of(row * cols, cols), cols),
                    kernel * LANES : (kernel + 1) * LANES,
                ] = made[kernel * cols : (kernel + 1) * cols]
        return carry

    lax.fori_loop(0, rows // group, some_rows, 0)


def fill_bands(taps, bands, cols):
    rows, kernels = taps.shape[0], taps.shape[1]

    def one_row(row, carry):
        level = jnp.broadcast_to(taps[row][:, None, :], (kernels, cols, LANES))
        slanted = pltpu.roll(level, 0, 2, stride=1, stride_axis=1)
        bands[row] = slanted.reshape(kernels * cols, LANES).astype(bands.dtype)
        return carry

    lax.fori_loop(0, rows, one_row, 0)


def mixed_back(spread, weight):
    total = None
    for kernel in range(weight.shape[0]):
        term = lax.dot_general(
            spread[:, kernel * LANES : (kernel + 1) * LANES],
            weight[kernel],
            (((1,), (1,)), ((), ())),
            preferred_element_type=jnp.float32,
        )
        total = term if total is None else total + term
    return total


def whole_kernel(
    scale, fields, cotangent, weight_one, weight_two, taps_ahead, taps_back,
    output, dfields, grads,
    bands_ahead, bands_back, extended, u_one, u_two, v_vals, slope_one, dhidden, terms,
    own, first_cols, last_cols, west, east, row_in, halo_send_sem, halo_recv_sem, *scratch
):
    rows, cols, channels = fields.shape
    flat = (rows * cols, channels)
    halo = (own, first_cols, last_cols, west, east, row_in, halo_send_sem, halo_recv_sem)
    here = coordinates()
    barrier = pltpu.get_barrier_semaphore()
    awaited = greet_halo(barrier) + greet_reducers(here, barrier)

    halo_prepare(0, fields[...].astype(jnp.float32), halo)
    extended[...] = jnp.zeros(extended.shape, extended.dtype)
    fill_bands(taps_ahead, bands_ahead, cols)
    pl.semaphore_wait(barrier, awaited)
    halo_send(0, halo)
    fill_bands(taps_back, bands_back, cols)
    halo_receive(0, halo, extended)

    apply_bands(bands_ahead, extended, u_one)
    mix_one = weight_one[...].reshape(-1, channels)
    pre = jnp.dot(u_one[...], mix_one, preferred_element_type=jnp.float32)
    value, slope = gelu_parts(pre)
    slope_one[...] = slope
    hidden = fields[...].astype(jnp.float32) + value.reshape(rows, cols, channels)
    halo_prepare(1, hidden, halo)
    halo_send(1, halo)
    halo_receive(1, halo, extended)

    apply_bands(bands_ahead, extended, u_two)
    mix_two = weight_two[...].reshape(-1, channels)
    pre = jnp.dot(u_two[...], mix_two, preferred_element_type=jnp.float32)
    value, slope = gelu_parts(pre)
    upstream = cotangent[...].astype(jnp.float32)
    dconv = upstream * slope.reshape(rows, cols, channels)
    halo_prepare(2, dconv, halo)
    halo_send(2, halo)
    output[...] = (
        own[1].astype(jnp.float32) + value.reshape(rows, cols, channels)
    ).astype(output.dtype)
    terms[1] = lax.dot_general(
        u_two[...], own[2].reshape(flat), (((0,), (0,)), ((), ())),
        preferred_element_type=jnp.float32,
    ).reshape(terms.shape[1:])
    halo_receive(2, halo, extended)

    apply_bands(bands_back, extended, v_vals)
    arrived = upstream.reshape(flat) + mixed_back(v_vals, weight_two)
    dhidden[...] = arrived
    halo_prepare(3, (arrived * slope_one[...]).reshape(rows, cols, channels), halo)
    halo_send(3, halo)
    terms[0] = lax.dot_general(
        u_one[...], own[3].reshape(flat), (((0,), (0,)), ((), ())),
        preferred_element_type=jnp.float32,
    ).reshape(terms.shape[1:])

    def last_gradient():
        halo_receive(3, halo, extended)
        apply_bands(bands_back, extended, v_vals)
        total = dhidden[...] + mixed_back(v_vals, weight_one)
        dfields[...] = total.reshape(rows, cols, channels).astype(dfields.dtype)

    reduce_everywhere(here, terms, grads, scale, scratch, last_gradient)
    for stage in range(own.shape[0]):
        for copy in halo_outgoing(stage, halo):
            copy.wait_send()


def tap_lanes(taps):
    kernels, rows, row_taps, lon_taps = taps.shape
    lead = RIM + lon_taps // 2
    period = 4 * RIM
    spaced = jnp.pad(
        taps.transpose(1, 0, 2, 3).astype(jnp.float32),
        ((0, 0), (0, RING - kernels), (0, 0), (0, period - lon_taps)),
    ).reshape(rows, RING, row_taps * period)
    return jnp.pad(spaced, ((0, 0), (0, 0), (lead, LANES - lead - row_taps * period)))


def body(fields, weight_one, weight_two, basis_raw, widths, cotangent):
    rows, cols, channels = fields.shape
    kernels = weight_one.shape[0]
    basis = padded_basis(basis_raw, widths)
    first_row = lax.axis_index("lat") * rows
    ahead = lax.dynamic_slice_in_dim(basis, first_row + 2, rows, 1)
    around = lax.dynamic_slice_in_dim(basis, first_row + 1, rows + 2, 1)
    back = jnp.stack(
        [around[:, side : side + rows, 2 - side, ::-1] for side in range(3)], axis=2
    )
    scale = 1.0 / math.sqrt(rows * lax.axis_size("lat") * cols * lax.axis_size("lon"))
    grad_rows = kernels * channels // RING
    low, high = jnp.bfloat16, jnp.float32
    height = (rows + 3) * (cols + 2 * RIM)
    stages = 4
    scratch = [
        pltpu.VMEM((rows, RING * cols, LANES), low),
        pltpu.VMEM((rows, RING * cols, LANES), low),
        pltpu.VMEM((height, channels), low),
        pltpu.VMEM((rows * cols, kernels * channels), low),
        pltpu.VMEM((rows * cols, kernels * channels), low),
        pltpu.VMEM((rows * cols, kernels * channels), low),
        pltpu.VMEM((rows * cols, channels), high),
        pltpu.VMEM((rows * cols, channels), high),
        pltpu.VMEM((2, RING, grad_rows, channels), high),
        pltpu.VMEM((stages, rows, cols, channels), low),
        pltpu.VMEM((stages, rows, RIM, channels), low),
        pltpu.VMEM((stages, rows, RIM, channels), low),
        pltpu.VMEM((stages, rows + 2, RIM, channels), low),
        pltpu.VMEM((stages, rows + 2, RIM, channels), low),
        pltpu.VMEM((stages, 2, cols, channels), low),
        pltpu.SemaphoreType.DMA((stages, 8)),
        pltpu.SemaphoreType.DMA((stages, 8)),
    ] + reduce_scratch(grad_rows, channels)
    output, dfields, grads = pl.pallas_call(
        functools.partial(whole_kernel, scale),
        out_shape=(
            jax.ShapeDtypeStruct(fields.shape, low),
            jax.ShapeDtypeStruct(fields.shape, low),
            jax.ShapeDtypeStruct((2, RING, grad_rows, channels), low),
        ),
        in_specs=[pl.BlockSpec(memory_space=pltpu.VMEM)] * 6,
        out_specs=(pl.BlockSpec(memory_space=pltpu.VMEM),) * 3,
        scratch_shapes=scratch,
        compiler_params=pltpu.CompilerParams(collective_id=0, has_side_effects=True),
    )(fields, cotangent, weight_one, weight_two, tap_lanes(ahead), tap_lanes(back))
    grads = grads.astype(jnp.float32).reshape(2, kernels, channels, channels)
    return output, dfields, grads[0], grads[1]


def solution(mesh):
    placed = (P("lat", "lon", None), P(), P(), P(), P(), P("lat", "lon", None))
    return jax.shard_map(
        body,
        mesh=mesh,
        in_specs=placed,
        out_specs=(P("lat", "lon", None), P("lat", "lon", None), P(), P()),
        check_vma=False,
    )
```

```python
import functools
import math

import jax
import jax.numpy as jnp
from jax import lax
from jax.experimental import pallas as pl
from jax.experimental.pallas import tpu as pltpu
from jax.sharding import PartitionSpec as P

MESH = pl.DeviceIdType.MESH
RING = 8
RIM = 8
LANES = 128
GELU_SLOPE = math.sqrt(2.0 / math.pi)
GELU_CUBIC = 0.044715


def padded_basis(basis_raw, widths):
    tap_count = basis_raw.shape[3]
    reach = (tap_count - 1) // 2
    distance = jnp.abs(jnp.arange(tap_count, dtype=jnp.int32) - reach)
    inside = (distance[None, :] <= widths[:, None]).astype(jnp.bfloat16)
    masked = basis_raw * inside[None, :, None, :]
    top_rows = masked[:, 0:1, ::-1, :]
    bottom = masked[:, -1:, ::-1, :]
    zero_row = jnp.zeros_like(top_rows)
    return jnp.concatenate([zero_row, top_rows, masked, bottom, zero_row], axis=1)


def coordinates():
    lat = lax.axis_index("lat")
    lon = lax.axis_index("lon")
    core = lax.rem(lon, 2)
    z = lax.rem(lax.div(lon, 2), RING)
    x = lax.rem(lax.div(lon, 2 * RING), RING)
    y = lat * 2 + lax.div(lon, 2 * RING * RING)
    return core, x, y, z


def device_at(core, x, y, z):
    return (lax.div(y, 2), lax.rem(y, 2) * (2 * RING * RING) + x * (2 * RING) + z * 2 + core)


def ring_peer(here, stage, step):
    core, x, y, z = here
    other = 1 - core
    on_x, on_y, on_z = ((other, core, 0), (0, other, core), (core, 0, other))[stage]
    return device_at(
        core,
        lax.rem(x + step * on_x, RING),
        lax.rem(y + step * on_y, RING),
        lax.rem(z + step * on_z, RING),
    )


def ring_index(here, stage):
    core, x, y, z = here
    first, second = ((x, y), (y, z), (z, x))[stage]
    return first * (1 - core) + second * core


def partner_of(here):
    core, x, y, z = here
    return device_at(1 - core, x, y, z)


def greet_reducers(here, barrier):
    pl.semaphore_signal(barrier, inc=1, device_id=partner_of(here), device_id_type=MESH)
    for stage in range(3):

        def greet(step, carry, stage=stage):
            pl.semaphore_signal(
                barrier, inc=1, device_id=ring_peer(here, stage, step), device_id_type=MESH
            )
            return carry

        lax.fori_loop(1, RING, greet, 0)
    return 1 + 3 * (RING - 1)


FAR_FIRST = (4, 3, 5, 2, 6, 1, 7)
NEAR_FIRST = (1, 7, 2, 6, 3, 5, 4)


class Chain:
    def __init__(self, which, here, terms, result, scale, scratch):
        (self.pair_out, self.pair_in, self.halves, self.wide_out, self.wide_in, self.middle,
         self.last, self.chunk, self.other_half) = (ref.at[which] for ref in scratch[:9])
        self.pair_send, self.pair_recv, self.sends, self.recvs = (
            ref.at[which] for ref in scratch[9:]
        )
        self.here, self.terms, self.result, self.scale = here, terms.at[which], result, scale
        self.core = here[0]
        self.at = [ring_index(here, axis) for axis in range(3)]

    def pair_copy(self, source, target, slot):
        return pltpu.make_async_remote_copy(
            src_ref=source, dst_ref=target, send_sem=self.pair_send.at[slot],
            recv_sem=self.pair_recv.at[slot], device_id=partner_of(self.here),
            device_id_type=MESH,
        )

    def swap(self):
        return self.pair_copy(self.pair_out, self.pair_in, RING)

    def across(self, step):
        return self.pair_copy(self.chunk.at[step], self.other_half.at[step], step)

    def ring_copy(self, stage, axis, source, landing, step):
        return pltpu.make_async_remote_copy(
            src_ref=source, dst_ref=landing.at[step], send_sem=self.sends.at[stage, step],
            recv_sem=self.recvs.at[stage, step],
            device_id=ring_peer(self.here, axis, step), device_id_type=MESH,
        )

    def wide_copy(self, step):
        source = self.wide_out.at[lax.rem(self.at[0] + step, RING)]
        return self.ring_copy(0, 0, source, self.wide_in, step)

    def middle_copy(self, step):
        return self.ring_copy(1, 1, self.middle.at[0], self.middle, step)

    def last_copy(self, step):
        return self.ring_copy(2, 2, self.last.at[0], self.last, step)

    def chunk_copy(self, step):
        return self.ring_copy(3, 0, self.chunk.at[0], self.chunk, step)

    def begin(self):
        self.pair_out[...] = self.terms[1 - self.core].astype(jnp.bfloat16)
        self.swap().start()

    def scatter(self):
        self.swap().wait_recv()
        both = self.terms[self.core] + self.pair_in[...].astype(jnp.float32)
        self.halves[...] = both
        self.wide_out[...] = both.astype(jnp.bfloat16)
        for step in FAR_FIRST:
            self.wide_copy(step).start()

    def sum_first(self):
        total = self.halves[self.at[0]]
        for step in NEAR_FIRST:
            self.wide_copy(step).wait_recv()
            total = total + self.wide_in[step].astype(jnp.float32)
        self.middle[0] = total.astype(jnp.bfloat16)
        for step in FAR_FIRST:
            self.middle_copy(step).start()

    def in_order(self, landing, axis):
        total = None
        for source in range(RING):
            term = landing[lax.rem(self.at[axis] - source + RING, RING)].astype(jnp.float32)
            total = term if total is None else total + term
        return total

    def sum_second(self):
        for step in NEAR_FIRST:
            self.middle_copy(step).wait_recv()
        self.last[0] = self.in_order(self.middle, 1).astype(jnp.bfloat16)
        for step in FAR_FIRST:
            self.last_copy(step).start()

    def sum_third(self):
        for step in NEAR_FIRST:
            self.last_copy(step).wait_recv()
        self.chunk[0] = (self.in_order(self.last, 2) * self.scale).astype(jnp.bfloat16)
        for step in FAR_FIRST:
            self.chunk_copy(step).start()
        self.across(0).start()

    def gather(self):
        core, x, y, _ = self.here
        for step in NEAR_FIRST:
            self.chunk_copy(step).wait_recv()
            self.across(step).start()
        for source in range(RING):
            self.result[core, source] = self.chunk[
                lax.rem(self.at[0] - source + RING, RING)
            ].astype(jnp.float32)
        at_partner = y * (1 - core) + x * core
        for step in (0,) + NEAR_FIRST:
            self.across(step).wait_recv()
        for source in range(RING):
            self.result[1 - core, source] = self.other_half[
                lax.rem(at_partner - source + RING, RING)
            ].astype(jnp.float32)

    def drain(self):
        self.swap().wait_send()
        for step in range(RING):
            self.across(step).wait_send()

        def one(step, carry):
            self.wide_copy(step).wait_send()
            self.middle_copy(step).wait_send()
            self.last_copy(step).wait_send()
            self.chunk_copy(step).wait_send()
            return carry

        lax.fori_loop(1, RING, one, 0)


def reduce_scratch(rows, lanes):
    low, high = jnp.bfloat16, jnp.float32
    kinds = [low, low, high, low, low, low, low, low, low]
    return [pltpu.VMEM((2, RING, rows, lanes), kind) for kind in kinds] + [
        pltpu.SemaphoreType.DMA((2, 1 + RING)),
        pltpu.SemaphoreType.DMA((2, 1 + RING)),
        pltpu.SemaphoreType.DMA((2, 4, RING)),
        pltpu.SemaphoreType.DMA((2, 4, RING)),
    ]


def gelu_parts(pre):
    square = pre * pre
    bent = jnp.tanh(GELU_SLOPE * pre * (1.0 + GELU_CUBIC * square))
    value = 0.5 * pre * (1.0 + bent)
    slope = 0.5 * (1.0 + bent) + 0.5 * pre * (1.0 - bent * bent) * GELU_SLOPE * (
        1.0 + 3.0 * GELU_CUBIC * square
    )
    return value, slope


def halo_devices():
    lat = lax.axis_index("lat")
    lon = lax.axis_index("lon")
    lats = lax.axis_size("lat")
    lons = lax.axis_size("lon")
    at_top = lax.div(lats - 1 - lat, lats - 1)
    at_bottom = lax.div(lat, lats - 1)
    right = lax.rem(lon + 1, lons)
    left = lax.rem(lon + lons - 1, lons)
    ends = []
    for at_end, step, row_slot in ((at_top, -1, 1 - at_top), (at_bottom, 1, at_bottom)):
        far_lat = lat + step * (1 - at_end)
        turn = at_end * (lons // 2)
        ends.append(
            (
                row_slot,
                (far_lat, lax.rem(lon + turn, lons)),
                (far_lat, lax.rem(right + turn, lons)),
                (far_lat, lax.rem(left + turn, lons)),
            )
        )
    return (lat, right), (lat, left), ends


def greet_halo(barrier):
    right, left, ends = halo_devices()
    others = [right, left]
    for _, straight, to_right, to_left in ends:
        others += [straight, to_right, to_left]
    for other in others:
        pl.semaphore_signal(barrier, inc=1, device_id=other, device_id_type=MESH)
    return len(others)


def halo_outgoing(stage, halo):
    own, first_cols, last_cols, west, east, row_in, send_sem, recv_sem = halo
    rows = own.shape[1]
    right, left, ends = halo_devices()
    count = 0

    def copy(source, target, slot, device):
        nonlocal count
        count += 1
        return pltpu.make_async_remote_copy(
            src_ref=source, dst_ref=target, send_sem=send_sem.at[stage, count - 1],
            recv_sem=recv_sem.at[stage, slot], device_id=device, device_id_type=MESH,
        )

    outgoing = []
    for (slot, straight, to_right, to_left), row in zip(ends, (0, rows - 1)):
        edge = slot * (rows + 1)
        outgoing += [
            copy(last_cols.at[stage, row], west.at[stage, edge], 4 + slot, to_right),
            copy(first_cols.at[stage, row], east.at[stage, edge], 6 + slot, to_left),
            copy(own.at[stage, row], row_in.at[stage, slot], 2 + slot, straight),
        ]
    inner = pl.ds(1, rows)
    outgoing += [
        copy(last_cols.at[stage], west.at[stage, inner], 0, right),
        copy(first_cols.at[stage], east.at[stage, inner], 1, left),
    ]
    return outgoing


def halo_incoming(stage, halo):
    own, first_cols, last_cols, west, east, row_in, send_sem, recv_sem = halo
    rows = own.shape[1]
    right, left, _ = halo_devices()

    def copy(source, target, slot, device):
        return pltpu.make_async_remote_copy(
            src_ref=source, dst_ref=target, send_sem=send_sem.at[stage, slot],
            recv_sem=recv_sem.at[stage, slot], device_id=device, device_id_type=MESH,
        )

    inner = pl.ds(1, rows)
    incoming = [
        copy(last_cols.at[stage], west.at[stage, inner], 0, right),
        copy(first_cols.at[stage], east.at[stage, inner], 1, left),
    ]
    for slot in range(2):
        edge = slot * (rows + 1)
        incoming += [
            copy(own.at[stage, 0], row_in.at[stage, slot], 2 + slot, right),
            copy(last_cols.at[stage, 0], west.at[stage, edge], 4 + slot, right),
            copy(first_cols.at[stage, 0], east.at[stage, edge], 6 + slot, right),
        ]
    return incoming


def halo_prepare(stage, field, halo):
    own, first_cols, last_cols = halo[:3]
    own[stage] = field.astype(own.dtype)
    first_cols[stage] = field[:, :RIM].astype(own.dtype)
    last_cols[stage] = field[:, -RIM:].astype(own.dtype)


def halo_send(stage, halo):
    for copy in halo_outgoing(stage, halo):
        copy.start()


def halo_receive(stage, halo, extended):
    own, _, _, west, east, row_in = halo[:6]
    rows, cols = own.shape[1], own.shape[2]
    period = cols + 2 * RIM

    for row in range(rows):
        start = (row + 1) * period + 2 * RIM
        extended[start : start + cols] = own[stage, row]
    for copy in halo_incoming(stage, halo):
        copy.wait_recv()
    for slot in range(2):
        start = slot * (rows + 1) * period + 2 * RIM
        extended[start : start + cols] = row_in[stage, slot]
    west_rim = west[stage].astype(jnp.float32)
    east_rim = east[stage].astype(jnp.float32)
    blank = jnp.zeros((1, RIM, LANES), jnp.float32)
    rims = jnp.concatenate(
        [
            jnp.concatenate([blank, east_rim], axis=0),
            jnp.concatenate([west_rim, blank], axis=0),
        ],
        axis=1,
    ).astype(own.dtype)
    for row in range(rows + 3):
        extended[row * period : row * period + 2 * RIM] = rims[row]


def apply_bands(bands, extended, spread):
    rows, height = bands.shape[0], bands.shape[1]
    kernels = spread.shape[1] // LANES
    cols = spread.shape[0] // rows
    period = cols + 2 * RIM
    group = 4

    def some_rows(index, carry):
        for part in range(group):
            row = index * group + part
            window = extended[pl.ds(pl.multiple_of(row * period, period), LANES)]
            made = jnp.dot(
                bands[row], window, preferred_element_type=jnp.float32
            ).astype(spread.dtype)
            for kernel in range(kernels):
                spread[
                    pl.ds(pl.multiple_of(row * cols, cols), cols),
                    kernel * LANES : (kernel + 1) * LANES,
                ] = made[kernel * cols : (kernel + 1) * cols]
        return carry

    lax.fori_loop(0, rows // group, some_rows, 0)


def fill_bands(taps, bands, cols):
    rows, kernels = taps.shape[0], taps.shape[1]

    def one_row(row, carry):
        level = jnp.broadcast_to(taps[row][:, None, :], (kernels, cols, LANES))
        slanted = pltpu.roll(level, 0, 2, stride=1, stride_axis=1)
        bands[row] = slanted.reshape(kernels * cols, LANES).astype(bands.dtype)
        return carry

    lax.fori_loop(0, rows, one_row, 0)


def mixed_back(spread, weight):
    total = None
    for kernel in range(weight.shape[0]):
        term = lax.dot_general(
            spread[:, kernel * LANES : (kernel + 1) * LANES],
            weight[kernel],
            (((1,), (1,)), ((), ())),
            preferred_element_type=jnp.float32,
        )
        total = term if total is None else total + term
    return total


def whole_kernel(
    scale, fields, cotangent, weight_one, weight_two, taps_ahead, taps_back,
    output, dfields, grad_one, grad_two,
    bands_ahead, bands_back, extended, u_one, u_two, v_vals, slope_one, dhidden, terms,
    own, first_cols, last_cols, west, east, row_in, halo_send_sem, halo_recv_sem, *scratch
):
    rows, cols, channels = fields.shape
    flat = (rows * cols, channels)
    halo = (own, first_cols, last_cols, west, east, row_in, halo_send_sem, halo_recv_sem)
    here = coordinates()
    chain_one = Chain(0, here, terms, grad_one, scale, scratch)
    chain_two = Chain(1, here, terms, grad_two, scale, scratch)
    barrier = pltpu.get_barrier_semaphore()
    awaited = greet_halo(barrier) + greet_reducers(here, barrier)

    halo_prepare(0, fields[...].astype(jnp.float32), halo)
    extended[...] = jnp.zeros(extended.shape, extended.dtype)
    fill_bands(taps_ahead, bands_ahead, cols)
    pl.semaphore_wait(barrier, awaited)
    halo_send(0, halo)
    fill_bands(taps_back, bands_back, cols)
    halo_receive(0, halo, extended)

    apply_bands(bands_ahead, extended, u_one)
    mix_one = weight_one[...].reshape(-1, channels)
    pre = jnp.dot(u_one[...], mix_one, preferred_element_type=jnp.float32)
    value, slope = gelu_parts(pre)
    slope_one[...] = slope
    hidden = fields[...].astype(jnp.float32) + value.reshape(rows, cols, channels)
    halo_prepare(1, hidden, halo)
    halo_send(1, halo)
    halo_receive(1, halo, extended)

    apply_bands(bands_ahead, extended, u_two)
    mix_two = weight_two[...].reshape(-1, channels)
    pre = jnp.dot(u_two[...], mix_two, preferred_element_type=jnp.float32)
    value, slope = gelu_parts(pre)
    upstream = cotangent[...].astype(jnp.float32)
    dconv = upstream * slope.reshape(rows, cols, channels)
    halo_prepare(2, dconv, halo)
    halo_send(2, halo)
    output[...] = (
        own[1].astype(jnp.float32) + value.reshape(rows, cols, channels)
    ).astype(output.dtype)
    terms[1] = lax.dot_general(
        u_two[...], own[2].reshape(flat), (((0,), (0,)), ((), ())),
        preferred_element_type=jnp.float32,
    ).reshape(terms.shape[1:])
    chain_two.begin()
    halo_receive(2, halo, extended)
    chain_two.scatter()

    apply_bands(bands_back, extended, v_vals)
    arrived = upstream.reshape(flat) + mixed_back(v_vals, weight_two)
    dhidden[...] = arrived
    dconv = (arrived * slope_one[...]).reshape(rows, cols, channels)
    own[3] = dconv.astype(own.dtype)
    terms[0] = lax.dot_general(
        u_one[...], own[3].reshape(flat), (((0,), (0,)), ((), ())),
        preferred_element_type=jnp.float32,
    ).reshape(terms.shape[1:])
    chain_one.begin()
    halo_prepare(3, dconv, halo)
    halo_send(3, halo)
    chain_two.sum_first()
    chain_one.scatter()
    chain_two.sum_second()

    halo_receive(3, halo, extended)
    apply_bands(bands_back, extended, v_vals)
    total = dhidden[...] + mixed_back(v_vals, weight_one)
    dfields[...] = total.reshape(rows, cols, channels).astype(dfields.dtype)

    chain_one.sum_first()
    chain_two.sum_third()
    chain_one.sum_second()
    chain_two.gather()
    chain_one.sum_third()
    chain_two.drain()
    chain_one.gather()
    chain_one.drain()
    for stage in range(own.shape[0]):
        for copy in halo_outgoing(stage, halo):
            copy.wait_send()


def tap_lanes(taps):
    kernels, rows, row_taps, lon_taps = taps.shape
    lead = RIM + lon_taps // 2
    period = 4 * RIM
    spaced = jnp.pad(
        taps.transpose(1, 0, 2, 3).astype(jnp.float32),
        ((0, 0), (0, RING - kernels), (0, 0), (0, period - lon_taps)),
    ).reshape(rows, RING, row_taps * period)
    return jnp.pad(spaced, ((0, 0), (0, 0), (lead, LANES - lead - row_taps * period)))


def body(fields, weight_one, weight_two, basis_raw, widths, cotangent):
    rows, cols, channels = fields.shape
    kernels = weight_one.shape[0]
    basis = padded_basis(basis_raw, widths)
    first_row = lax.axis_index("lat") * rows
    ahead = lax.dynamic_slice_in_dim(basis, first_row + 2, rows, 1)
    around = lax.dynamic_slice_in_dim(basis, first_row + 1, rows + 2, 1)
    back = jnp.stack(
        [around[:, side : side + rows, 2 - side, ::-1] for side in range(3)], axis=2
    )
    scale = 1.0 / math.sqrt(rows * lax.axis_size("lat") * cols * lax.axis_size("lon"))
    grad_rows = kernels * channels // (2 * RING)
    low, high = jnp.bfloat16, jnp.float32
    height = (rows + 3) * (cols + 2 * RIM)
    stages = 4
    scratch = [
        pltpu.VMEM((rows, RING * cols, LANES), low),
        pltpu.VMEM((rows, RING * cols, LANES), low),
        pltpu.VMEM((height, channels), low),
        pltpu.VMEM((rows * cols, kernels * channels), low),
        pltpu.VMEM((rows * cols, kernels * channels), low),
        pltpu.VMEM((rows * cols, kernels * channels), low),
        pltpu.VMEM((rows * cols, channels), high),
        pltpu.VMEM((rows * cols, channels), high),
        pltpu.VMEM((2, 2, RING, grad_rows, channels), high),
        pltpu.VMEM((stages, rows, cols, channels), low),
        pltpu.VMEM((stages, rows, RIM, channels), low),
        pltpu.VMEM((stages, rows, RIM, channels), low),
        pltpu.VMEM((stages, rows + 2, RIM, channels), low),
        pltpu.VMEM((stages, rows + 2, RIM, channels), low),
        pltpu.VMEM((stages, 2, cols, channels), low),
        pltpu.SemaphoreType.DMA((stages, 8)),
        pltpu.SemaphoreType.DMA((stages, 8)),
    ] + reduce_scratch(grad_rows, channels)
    wide = jax.ShapeDtypeStruct((2, RING, grad_rows, channels), high)
    output, dfields, grad_one, grad_two = pl.pallas_call(
        functools.partial(whole_kernel, scale),
        out_shape=(
            jax.ShapeDtypeStruct(fields.shape, low),
            jax.ShapeDtypeStruct(fields.shape, low),
            wide,
            wide,
        ),
        in_specs=[pl.BlockSpec(memory_space=pltpu.VMEM)] * 6,
        out_specs=(pl.BlockSpec(memory_space=pltpu.VMEM),) * 4,
        scratch_shapes=scratch,
        compiler_params=pltpu.CompilerParams(collective_id=0, has_side_effects=True),
    )(fields, cotangent, weight_one, weight_two, tap_lanes(ahead), tap_lanes(back))
    shape = (kernels, channels, channels)
    return output, dfields, grad_one.reshape(shape), grad_two.reshape(shape)


def solution(mesh):
    placed = (P("lat", "lon", None), P(), P(), P(), P(), P("lat", "lon", None))
    return jax.shard_map(
        body,
        mesh=mesh,
        in_specs=placed,
        out_specs=(P("lat", "lon", None), P("lat", "lon", None), P(), P()),
        check_vma=False,
    )
```

```python
import math

import jax
import jax.numpy as jnp
from jax import lax
from jax.experimental import pallas as pl
from jax.experimental.pallas import tpu as pltpu
from jax.sharding import PartitionSpec as P

MESH = pl.DeviceIdType.MESH
RING = 8
RIM = 8
LANES = 128
GELU_SLOPE = math.sqrt(2.0 / math.pi)
GELU_CUBIC = 0.044715


def coordinates():
    lat = lax.axis_index("lat")
    lon = lax.axis_index("lon")
    core = lax.rem(lon, 2)
    z = lax.rem(lax.div(lon, 2), RING)
    x = lax.rem(lax.div(lon, 2 * RING), RING)
    y = lat * 2 + lax.div(lon, 2 * RING * RING)
    return core, x, y, z


def device_at(core, x, y, z):
    return (lax.div(y, 2), lax.rem(y, 2) * (2 * RING * RING) + x * (2 * RING) + z * 2 + core)


def ring_peer(here, stage, step):
    core, x, y, z = here
    other = 1 - core
    on_x, on_y, on_z = ((other, core, 0), (0, other, core), (core, 0, other))[stage]
    return device_at(
        core,
        lax.rem(x + step * on_x, RING),
        lax.rem(y + step * on_y, RING),
        lax.rem(z + step * on_z, RING),
    )


def ring_index(here, stage):
    core, x, y, z = here
    first, second = ((x, y), (y, z), (z, x))[stage]
    return first * (1 - core) + second * core


def partner_of(here):
    core, x, y, z = here
    return device_at(1 - core, x, y, z)


def greet_reducers(here, barrier):
    pl.semaphore_signal(barrier, inc=1, device_id=partner_of(here), device_id_type=MESH)
    for stage in range(3):

        def greet(step, carry, stage=stage):
            pl.semaphore_signal(
                barrier, inc=1, device_id=ring_peer(here, stage, step), device_id_type=MESH
            )
            return carry

        lax.fori_loop(1, RING, greet, 0)
    return 1 + 3 * (RING - 1)


FAR_FIRST = (4, 3, 5, 2, 6, 1, 7)
NEAR_FIRST = (1, 7, 2, 6, 3, 5, 4)


class Chain:
    def __init__(self, which, here, terms, result, scratch):
        (self.pair_out, self.pair_in, self.halves, self.wide_out, self.wide_in, self.middle,
         self.last, self.chunk, self.other_half) = (ref.at[which] for ref in scratch[:9])
        self.pair_send, self.pair_recv, self.sends, self.recvs = (
            ref.at[which] for ref in scratch[9:]
        )
        self.here, self.terms, self.result = here, terms.at[which], result
        self.core = here[0]
        self.at = [ring_index(here, axis) for axis in range(3)]

    def pair_copy(self, source, target, slot):
        return pltpu.make_async_remote_copy(
            src_ref=source, dst_ref=target, send_sem=self.pair_send.at[slot],
            recv_sem=self.pair_recv.at[slot], device_id=partner_of(self.here),
            device_id_type=MESH,
        )

    def swap(self):
        return self.pair_copy(self.pair_out, self.pair_in, RING)

    def across(self, step):
        return self.pair_copy(self.chunk.at[step], self.other_half.at[step], step)

    def ring_copy(self, stage, axis, source, landing, step):
        return pltpu.make_async_remote_copy(
            src_ref=source, dst_ref=landing.at[step], send_sem=self.sends.at[stage, step],
            recv_sem=self.recvs.at[stage, step],
            device_id=ring_peer(self.here, axis, step), device_id_type=MESH,
        )

    def wide_copy(self, step):
        source = self.wide_out.at[lax.rem(self.at[0] + step, RING)]
        return self.ring_copy(0, 0, source, self.wide_in, step)

    def middle_copy(self, step):
        return self.ring_copy(1, 1, self.middle.at[0], self.middle, step)

    def last_copy(self, step):
        return self.ring_copy(2, 2, self.last.at[0], self.last, step)

    def chunk_copy(self, step):
        return self.ring_copy(3, 0, self.chunk.at[0], self.chunk, step)

    def begin(self):
        self.pair_out[...] = self.terms[1 - self.core].astype(jnp.bfloat16)
        self.swap().start()

    def scatter(self):
        self.swap().wait_recv()
        both = self.terms[self.core] + self.pair_in[...].astype(jnp.float32)
        self.halves[...] = both
        self.wide_out[...] = both.astype(jnp.bfloat16)
        for step in FAR_FIRST:
            self.wide_copy(step).start()

    def sum_first(self):
        total = self.halves[self.at[0]]
        for step in NEAR_FIRST:
            self.wide_copy(step).wait_recv()
            total = total + self.wide_in[step].astype(jnp.float32)
        self.middle[0] = total.astype(jnp.bfloat16)
        for step in FAR_FIRST:
            self.middle_copy(step).start()

    def in_order(self, landing, axis):
        total = None
        for source in range(RING):
            term = landing[lax.rem(self.at[axis] - source + RING, RING)].astype(jnp.float32)
            total = term if total is None else total + term
        return total

    def sum_second(self):
        for step in NEAR_FIRST:
            self.middle_copy(step).wait_recv()
        self.last[0] = self.in_order(self.middle, 1).astype(jnp.bfloat16)
        for step in FAR_FIRST:
            self.last_copy(step).start()

    def sum_third(self):
        for step in NEAR_FIRST:
            self.last_copy(step).wait_recv()
        self.chunk[0] = self.in_order(self.last, 2).astype(jnp.bfloat16)
        for step in FAR_FIRST:
            self.chunk_copy(step).start()
        self.across(0).start()

    def gather(self):
        core, x, y, _ = self.here
        for step in NEAR_FIRST:
            self.chunk_copy(step).wait_recv()
            self.across(step).start()
        for source in range(RING):
            self.result[core, source] = self.chunk[
                lax.rem(self.at[0] - source + RING, RING)
            ].astype(jnp.float32)
        at_partner = y * (1 - core) + x * core
        for step in (0,) + NEAR_FIRST:
            self.across(step).wait_recv()
        for source in range(RING):
            self.result[1 - core, source] = self.other_half[
                lax.rem(at_partner - source + RING, RING)
            ].astype(jnp.float32)

    def drain(self):
        self.swap().wait_send()
        for step in range(RING):
            self.across(step).wait_send()

        def one(step, carry):
            self.wide_copy(step).wait_send()
            self.middle_copy(step).wait_send()
            self.last_copy(step).wait_send()
            self.chunk_copy(step).wait_send()
            return carry

        lax.fori_loop(1, RING, one, 0)


def reduce_scratch(rows, lanes):
    low, high = jnp.bfloat16, jnp.float32
    kinds = [low, low, high, low, low, low, low, low, low]
    return [pltpu.VMEM((2, RING, rows, lanes), kind) for kind in kinds] + [
        pltpu.SemaphoreType.DMA((2, 1 + RING)),
        pltpu.SemaphoreType.DMA((2, 1 + RING)),
        pltpu.SemaphoreType.DMA((2, 4, RING)),
        pltpu.SemaphoreType.DMA((2, 4, RING)),
    ]


def gelu_parts(pre):
    square = pre * pre
    bent = jnp.tanh(GELU_SLOPE * pre * (1.0 + GELU_CUBIC * square))
    value = 0.5 * pre * (1.0 + bent)
    slope = 0.5 * (1.0 + bent) + 0.5 * pre * (1.0 - bent * bent) * GELU_SLOPE * (
        1.0 + 3.0 * GELU_CUBIC * square
    )
    return value, slope


def halo_devices():
    lat = lax.axis_index("lat")
    lon = lax.axis_index("lon")
    lats = lax.axis_size("lat")
    lons = lax.axis_size("lon")
    at_top = lax.div(lats - 1 - lat, lats - 1)
    at_bottom = lax.div(lat, lats - 1)
    right = lax.rem(lon + 1, lons)
    left = lax.rem(lon + lons - 1, lons)
    ends = []
    for at_end, step, row_slot in ((at_top, -1, 1 - at_top), (at_bottom, 1, at_bottom)):
        far_lat = lat + step * (1 - at_end)
        turn = at_end * (lons // 2)
        ends.append(
            (
                row_slot,
                (far_lat, lax.rem(lon + turn, lons)),
                (far_lat, lax.rem(right + turn, lons)),
                (far_lat, lax.rem(left + turn, lons)),
            )
        )
    return (lat, right), (lat, left), ends


def greet_halo(barrier):
    right, left, ends = halo_devices()
    others = [right, left]
    for _, straight, to_right, to_left in ends:
        others += [straight, to_right, to_left]
    for other in others:
        pl.semaphore_signal(barrier, inc=1, device_id=other, device_id_type=MESH)
    return len(others)


def halo_outgoing(stage, halo):
    own, first_cols, last_cols, west, east, row_in, send_sem, recv_sem = halo
    rows = own.shape[1]
    right, left, ends = halo_devices()
    count = 0

    def copy(source, target, slot, device):
        nonlocal count
        count += 1
        return pltpu.make_async_remote_copy(
            src_ref=source, dst_ref=target, send_sem=send_sem.at[stage, count - 1],
            recv_sem=recv_sem.at[stage, slot], device_id=device, device_id_type=MESH,
        )

    outgoing = []
    for (slot, straight, to_right, to_left), row in zip(ends, (0, rows - 1)):
        edge = slot * (rows + 1)
        outgoing += [
            copy(last_cols.at[stage, row], west.at[stage, edge], 4 + slot, to_right),
            copy(first_cols.at[stage, row], east.at[stage, edge], 6 + slot, to_left),
            copy(own.at[stage, row], row_in.at[stage, slot], 2 + slot, straight),
        ]
    inner = pl.ds(1, rows)
    outgoing += [
        copy(last_cols.at[stage], west.at[stage, inner], 0, right),
        copy(first_cols.at[stage], east.at[stage, inner], 1, left),
    ]
    return outgoing


def halo_incoming(stage, halo):
    own, first_cols, last_cols, west, east, row_in, send_sem, recv_sem = halo
    rows = own.shape[1]
    right, left, _ = halo_devices()

    def copy(source, target, slot, device):
        return pltpu.make_async_remote_copy(
            src_ref=source, dst_ref=target, send_sem=send_sem.at[stage, slot],
            recv_sem=recv_sem.at[stage, slot], device_id=device, device_id_type=MESH,
        )

    inner = pl.ds(1, rows)
    incoming = [
        copy(last_cols.at[stage], west.at[stage, inner], 0, right),
        copy(first_cols.at[stage], east.at[stage, inner], 1, left),
    ]
    for slot in range(2):
        edge = slot * (rows + 1)
        incoming += [
            copy(own.at[stage, 0], row_in.at[stage, slot], 2 + slot, right),
            copy(last_cols.at[stage, 0], west.at[stage, edge], 4 + slot, right),
            copy(first_cols.at[stage, 0], east.at[stage, edge], 6 + slot, right),
        ]
    return incoming


def halo_prepare(stage, field, halo):
    own, first_cols, last_cols = halo[:3]
    own[stage] = field.astype(own.dtype)
    first_cols[stage] = field[:, :RIM].astype(own.dtype)
    last_cols[stage] = field[:, -RIM:].astype(own.dtype)


def halo_send(stage, halo):
    for copy in halo_outgoing(stage, halo):
        copy.start()


def halo_receive(stage, halo, extended):
    own, _, _, west, east, row_in = halo[:6]
    rows, cols = own.shape[1], own.shape[2]
    period = cols + 2 * RIM

    for row in range(rows):
        start = (row + 1) * period + 2 * RIM
        extended[start : start + cols] = own[stage, row]
    for copy in halo_incoming(stage, halo):
        copy.wait_recv()
    for slot in range(2):
        start = slot * (rows + 1) * period + 2 * RIM
        extended[start : start + cols] = row_in[stage, slot]
    west_rim = west[stage].astype(jnp.float32)
    east_rim = east[stage].astype(jnp.float32)
    blank = jnp.zeros((1, RIM, LANES), jnp.float32)
    rims = jnp.concatenate(
        [
            jnp.concatenate([blank, east_rim], axis=0),
            jnp.concatenate([west_rim, blank], axis=0),
        ],
        axis=1,
    ).astype(own.dtype)
    for row in range(rows + 3):
        extended[row * period : row * period + 2 * RIM] = rims[row]


def apply_bands(bands, extended, spread):
    rows = bands.shape[0]
    kernels = spread.shape[1] // LANES
    cols = spread.shape[0] // rows
    period = cols + 2 * RIM
    group = 4

    def some_rows(index, carry):
        for part in range(group):
            row = index * group + part
            window = extended[pl.ds(pl.multiple_of(row * period, period), LANES)]
            made = jnp.dot(
                bands[row], window, preferred_element_type=jnp.float32
            ).astype(spread.dtype)
            for kernel in range(kernels):
                spread[
                    pl.ds(pl.multiple_of(row * cols, cols), cols),
                    kernel * LANES : (kernel + 1) * LANES,
                ] = made[kernel * cols : (kernel + 1) * cols]
        return carry

    lax.fori_loop(0, rows // group, some_rows, 0)


def load_taps(basis, taps, first, at_top, at_bottom):
    kernels, _, row_taps, lon_taps = basis.shape
    rows = taps.shape[1] - 2
    low_end, high_end = row_taps - 1, 0
    taps[...] = jnp.zeros(taps.shape, taps.dtype)

    def one_kernel(kernel, carry):
        taps[kernel, 1 : rows + 1, :row_taps, :lon_taps] = basis[
            kernel, pl.ds(first, rows)
        ].astype(taps.dtype)
        above = basis[kernel, first - 1 + at_top].astype(taps.dtype)
        below = basis[kernel, first + rows - at_bottom].astype(taps.dtype)
        taps[kernel, 0, low_end : low_end + 1, :lon_taps] = jnp.where(
            at_top == 1, above[:1], above[low_end:]
        )
        taps[kernel, rows + 1, high_end : high_end + 1, :lon_taps] = jnp.where(
            at_bottom == 1, below[low_end:], below[:1]
        )
        return carry

    lax.fori_loop(0, kernels, one_kernel, 0)


def slant(lined, cols):
    kernels = lined.shape[0]
    level = jnp.broadcast_to(jnp.sum(lined, axis=1, keepdims=True), (kernels, cols, LANES))
    return pltpu.roll(level, 0, 2, stride=1, stride_axis=1).reshape(kernels * cols, LANES)


def fan_out(lined, start, stride):
    sublane = lax.broadcasted_iota(jnp.int32, lined.shape, 1)
    total = None
    for row_tap in range(3):
        moved = pltpu.roll(lined, (start + stride * row_tap) % LANES, 2)
        moved = jnp.where(sublane == row_tap, moved, 0.0)
        total = moved if total is None else total + moved
    return total


def within(shape, widths, row):
    offset = lax.broadcasted_iota(jnp.int32, shape, 2) - RIM // 2
    return jnp.abs(offset) <= widths[row]


def fill_ahead(taps, widths, bands, first, cols):
    rows = bands.shape[0]
    lead = RIM + RIM // 2

    def one_row(row, carry):
        seen = taps[:, row + 1]
        seen = jnp.where(within(seen.shape, widths, first + row), seen, 0.0)
        lined = fan_out(seen, lead, 4 * RIM)
        bands[row] = slant(lined, cols).astype(bands.dtype)
        return carry

    lax.fori_loop(0, rows, one_row, 0)


def fill_back(taps, widths, bands, first, last_row, cols):
    rows = bands.shape[0]
    lead = RIM + RIM // 2 + 2 * 4 * RIM + RIM
    kernels = taps.shape[0]
    lane_from = lax.broadcasted_iota(jnp.int32, (LANES, LANES), 0)
    lane_to = lax.broadcasted_iota(jnp.int32, (LANES, LANES), 1)
    turned = jnp.where(lane_from + lane_to == lead, 1.0, 0.0).astype(jnp.bfloat16)

    def one_row(row, carry):
        picked = None
        for row_tap in range(3):
            source = taps[:, row + 2 - row_tap]
            at = jnp.minimum(jnp.maximum(first + row + 1 - row_tap, 0), last_row)
            sublane = lax.broadcasted_iota(jnp.int32, source.shape, 1)
            kept = jnp.where(within(source.shape, widths, at) & (sublane == row_tap), source, 0.0)
            picked = kept if picked is None else picked + kept
        flipped = jnp.dot(
            picked.reshape(kernels * RING, LANES).astype(jnp.bfloat16), turned,
            preferred_element_type=jnp.float32,
        ).reshape(picked.shape)
        lined = fan_out(flipped, 0, LANES - 4 * RIM)
        bands[row] = slant(lined, cols).astype(bands.dtype)
        return carry

    lax.fori_loop(0, rows, one_row, 0)


def mixed_back(spread, weight):
    total = None
    for kernel in range(weight.shape[0]):
        term = lax.dot_general(
            spread[:, kernel * LANES : (kernel + 1) * LANES],
            weight[kernel],
            (((1,), (1,)), ((), ())),
            preferred_element_type=jnp.float32,
        )
        total = term if total is None else total + term
    return total


def whole_kernel(
    fields, cotangent, weight_one, weight_two, basis, widths,
    output, dfields, grad_one, grad_two,
    taps, bands_ahead, bands_back, extended, u_one, u_two, v_vals, slope_one, dhidden, terms,
    own, first_cols, last_cols, west, east, row_in, halo_send_sem, halo_recv_sem, *scratch
):
    rows, cols, channels = fields.shape
    flat = (rows * cols, channels)
    halo = (own, first_cols, last_cols, west, east, row_in, halo_send_sem, halo_recv_sem)
    here = coordinates()
    chain_one = Chain(0, here, terms, grad_one, scratch)
    chain_two = Chain(1, here, terms, grad_two, scratch)
    barrier = pltpu.get_barrier_semaphore()
    awaited = greet_halo(barrier) + greet_reducers(here, barrier)

    halo_prepare(0, fields[...].astype(jnp.float32), halo)
    pl.semaphore_wait(barrier, awaited)
    halo_send(0, halo)
    lat, lats = lax.axis_index("lat"), lax.axis_size("lat")
    first = pl.multiple_of(lat * rows, rows)
    at_top, at_bottom = lax.div(lats - 1 - lat, lats - 1), lax.div(lat, lats - 1)
    extended[...] = jnp.zeros(extended.shape, extended.dtype)
    load_taps(basis, taps, first, at_top, at_bottom)
    fill_ahead(taps, widths, bands_ahead, first, cols)
    fill_back(taps, widths, bands_back, first, lats * rows - 1, cols)
    halo_receive(0, halo, extended)

    apply_bands(bands_ahead, extended, u_one)
    mix_one = weight_one[...].reshape(-1, channels)
    pre = jnp.dot(u_one[...], mix_one, preferred_element_type=jnp.float32)
    value, slope = gelu_parts(pre)
    slope_one[...] = slope
    hidden = fields[...].astype(jnp.float32) + value.reshape(rows, cols, channels)
    halo_prepare(1, hidden, halo)
    halo_send(1, halo)
    halo_receive(1, halo, extended)

    apply_bands(bands_ahead, extended, u_two)
    mix_two = weight_two[...].reshape(-1, channels)
    pre = jnp.dot(u_two[...], mix_two, preferred_element_type=jnp.float32)
    value, slope = gelu_parts(pre)
    upstream = cotangent[...].astype(jnp.float32)
    dconv = upstream * slope.reshape(rows, cols, channels)
    halo_prepare(2, dconv, halo)
    halo_send(2, halo)
    output[...] = (
        own[1].astype(jnp.float32) + value.reshape(rows, cols, channels)
    ).astype(output.dtype)
    terms[1] = lax.dot_general(
        u_two[...], own[2].reshape(flat), (((0,), (0,)), ((), ())),
        preferred_element_type=jnp.float32,
    ).reshape(terms.shape[1:])
    chain_two.begin()
    halo_receive(2, halo, extended)
    chain_two.scatter()

    apply_bands(bands_back, extended, v_vals)
    arrived = upstream.reshape(flat) + mixed_back(v_vals, weight_two)
    dhidden[...] = arrived
    dconv = (arrived * slope_one[...]).reshape(rows, cols, channels)
    own[3] = dconv.astype(own.dtype)
    terms[0] = lax.dot_general(
        u_one[...], own[3].reshape(flat), (((0,), (0,)), ((), ())),
        preferred_element_type=jnp.float32,
    ).reshape(terms.shape[1:])
    chain_one.begin()
    halo_prepare(3, dconv, halo)
    halo_send(3, halo)
    chain_two.sum_first()
    chain_one.scatter()
    chain_two.sum_second()

    halo_receive(3, halo, extended)
    apply_bands(bands_back, extended, v_vals)
    total = dhidden[...] + mixed_back(v_vals, weight_one)
    dfields[...] = total.reshape(rows, cols, channels).astype(dfields.dtype)

    chain_one.sum_first()
    chain_two.sum_third()
    chain_one.sum_second()
    chain_two.gather()
    chain_one.sum_third()
    chain_two.drain()
    chain_one.gather()
    chain_one.drain()
    for stage in range(own.shape[0]):
        for copy in halo_outgoing(stage, halo):
            copy.wait_send()


def body(fields, weight_one, weight_two, basis_raw, widths, cotangent):
    rows, cols, channels = fields.shape
    kernels = weight_one.shape[0]
    scale = 1.0 / math.sqrt(rows * lax.axis_size("lat") * cols * lax.axis_size("lon"))
    grad_rows = kernels * channels // (2 * RING)
    low, high = jnp.bfloat16, jnp.float32
    height = (rows + 3) * (cols + 2 * RIM)
    stages = 4
    scratch = [
        pltpu.VMEM((kernels, rows + 2, RING, LANES), high),
        pltpu.VMEM((rows, kernels * cols, LANES), low),
        pltpu.VMEM((rows, kernels * cols, LANES), low),
        pltpu.VMEM((height, channels), low),
        pltpu.VMEM((rows * cols, kernels * channels), low),
        pltpu.VMEM((rows * cols, kernels * channels), low),
        pltpu.VMEM((rows * cols, kernels * channels), low),
        pltpu.VMEM((rows * cols, channels), high),
        pltpu.VMEM((rows * cols, channels), high),
        pltpu.VMEM((2, 2, RING, grad_rows, channels), high),
        pltpu.VMEM((stages, rows, cols, channels), low),
        pltpu.VMEM((stages, rows, RIM, channels), low),
        pltpu.VMEM((stages, rows, RIM, channels), low),
        pltpu.VMEM((stages, rows + 2, RIM, channels), low),
        pltpu.VMEM((stages, rows + 2, RIM, channels), low),
        pltpu.VMEM((stages, 2, cols, channels), low),
        pltpu.SemaphoreType.DMA((stages, 8)),
        pltpu.SemaphoreType.DMA((stages, 8)),
    ] + reduce_scratch(grad_rows, channels)
    wide = jax.ShapeDtypeStruct((2, RING, grad_rows, channels), high)
    output, dfields, grad_one, grad_two = pl.pallas_call(
        whole_kernel,
        out_shape=(
            jax.ShapeDtypeStruct(fields.shape, high),
            jax.ShapeDtypeStruct(fields.shape, high),
            wide,
            wide,
        ),
        in_specs=[pl.BlockSpec(memory_space=pltpu.VMEM)] * 5
        + [pl.BlockSpec(memory_space=pltpu.SMEM)],
        out_specs=(pl.BlockSpec(memory_space=pltpu.VMEM),) * 4,
        scratch_shapes=scratch,
        compiler_params=pltpu.CompilerParams(collective_id=0, has_side_effects=True),
    )(fields, cotangent, weight_one, weight_two, basis_raw, widths)
    shape = (kernels, channels, channels)
    return (
        output.astype(low),
        dfields.astype(low),
        grad_one.reshape(shape) * scale,
        grad_two.reshape(shape) * scale,
    )


def solution(mesh):
    placed = (P("lat", "lon", None), P(), P(), P(), P(), P("lat", "lon", None))
    return jax.shard_map(
        body,
        mesh=mesh,
        in_specs=placed,
        out_specs=(P("lat", "lon", None), P("lat", "lon", None), P(), P()),
        check_vma=False,
    )
```

```python
import math

import jax
import jax.numpy as jnp
from jax import lax
from jax.experimental import pallas as pl
from jax.experimental.pallas import tpu as pltpu
from jax.sharding import PartitionSpec as P

MESH = pl.DeviceIdType.MESH
RING = 8
RIM = 8
LANES = 128
PERIOD = 4 * RIM
LEAD = RIM + RIM // 2
GELU_SLOPE = math.sqrt(2.0 / math.pi)
GELU_CUBIC = 0.044715


def coordinates():
    lat = lax.axis_index("lat")
    lon = lax.axis_index("lon")
    core = lax.rem(lon, 2)
    z = lax.rem(lax.div(lon, 2), RING)
    x = lax.rem(lax.div(lon, 2 * RING), RING)
    y = lat * 2 + lax.div(lon, 2 * RING * RING)
    return core, x, y, z


def device_at(core, x, y, z):
    return (lax.div(y, 2), lax.rem(y, 2) * (2 * RING * RING) + x * (2 * RING) + z * 2 + core)


def ring_peer(here, stage, step):
    core, x, y, z = here
    other = 1 - core
    on_x, on_y, on_z = ((other, core, 0), (0, other, core), (core, 0, other))[stage]
    return device_at(
        core,
        lax.rem(x + step * on_x, RING),
        lax.rem(y + step * on_y, RING),
        lax.rem(z + step * on_z, RING),
    )


def ring_index(here, stage):
    core, x, y, z = here
    first, second = ((x, y), (y, z), (z, x))[stage]
    return first * (1 - core) + second * core


def partner_of(here):
    core, x, y, z = here
    return device_at(1 - core, x, y, z)


def greet_reducers(here, barrier):
    pl.semaphore_signal(barrier, inc=1, device_id=partner_of(here), device_id_type=MESH)
    for stage in range(3):

        def greet(step, carry, stage=stage):
            pl.semaphore_signal(
                barrier, inc=1, device_id=ring_peer(here, stage, step), device_id_type=MESH
            )
            return carry

        lax.fori_loop(1, RING, greet, 0)
    return 1 + 3 * (RING - 1)


FAR_FIRST = (4, 3, 5, 2, 6, 1, 7)
NEAR_FIRST = (1, 7, 2, 6, 3, 5, 4)


class Chain:
    def __init__(self, which, here, terms, result, scratch):
        (self.pair_out, self.pair_in, self.halves, self.wide_out, self.wide_in, self.middle,
         self.last, self.chunk, self.other_half) = (ref.at[which] for ref in scratch[:9])
        self.pair_send, self.pair_recv, self.sends, self.recvs = (
            ref.at[which] for ref in scratch[9:]
        )
        self.here, self.terms, self.result = here, terms.at[which], result
        self.core = here[0]
        self.at = [ring_index(here, axis) for axis in range(3)]

    def pair_copy(self, source, target, slot):
        return pltpu.make_async_remote_copy(
            src_ref=source, dst_ref=target, send_sem=self.pair_send.at[slot],
            recv_sem=self.pair_recv.at[slot], device_id=partner_of(self.here),
            device_id_type=MESH,
        )

    def swap(self):
        return self.pair_copy(self.pair_out, self.pair_in, RING)

    def across(self, step):
        return self.pair_copy(self.chunk.at[step], self.other_half.at[step], step)

    def ring_copy(self, stage, axis, source, landing, step):
        return pltpu.make_async_remote_copy(
            src_ref=source, dst_ref=landing.at[step], send_sem=self.sends.at[stage, step],
            recv_sem=self.recvs.at[stage, step],
            device_id=ring_peer(self.here, axis, step), device_id_type=MESH,
        )

    def wide_copy(self, step):
        source = self.wide_out.at[lax.rem(self.at[0] + step, RING)]
        return self.ring_copy(0, 0, source, self.wide_in, step)

    def middle_copy(self, step):
        return self.ring_copy(1, 1, self.middle.at[0], self.middle, step)

    def last_copy(self, step):
        return self.ring_copy(2, 2, self.last.at[0], self.last, step)

    def chunk_copy(self, step):
        return self.ring_copy(3, 0, self.chunk.at[0], self.chunk, step)

    def begin(self):
        self.pair_out[...] = self.terms[1 - self.core].astype(jnp.bfloat16)
        self.swap().start()

    def scatter(self):
        self.swap().wait_recv()
        both = self.terms[self.core] + self.pair_in[...].astype(jnp.float32)
        self.halves[...] = both
        self.wide_out[...] = both.astype(jnp.bfloat16)
        for step in FAR_FIRST:
            self.wide_copy(step).start()

    def sum_first(self):
        total = self.halves[self.at[0]]
        for step in NEAR_FIRST:
            self.wide_copy(step).wait_recv()
            total = total + self.wide_in[step].astype(jnp.float32)
        self.middle[0] = total.astype(jnp.bfloat16)
        for step in FAR_FIRST:
            self.middle_copy(step).start()

    def in_order(self, landing, axis):
        total = None
        for source in range(RING):
            term = landing[lax.rem(self.at[axis] - source + RING, RING)].astype(jnp.float32)
            total = term if total is None else total + term
        return total

    def sum_second(self):
        for step in NEAR_FIRST:
            self.middle_copy(step).wait_recv()
        self.last[0] = self.in_order(self.middle, 1).astype(jnp.bfloat16)
        for step in FAR_FIRST:
            self.last_copy(step).start()

    def sum_third(self):
        for step in NEAR_FIRST:
            self.last_copy(step).wait_recv()
        self.chunk[0] = self.in_order(self.last, 2).astype(jnp.bfloat16)
        for step in FAR_FIRST:
            self.chunk_copy(step).start()
        self.across(0).start()

    def gather(self):
        core, x, y, _ = self.here
        for step in NEAR_FIRST:
            self.chunk_copy(step).wait_recv()
            self.across(step).start()
        for source in range(RING):
            self.result[core, source] = self.chunk[
                lax.rem(self.at[0] - source + RING, RING)
            ].astype(jnp.float32)
        at_partner = y * (1 - core) + x * core
        for step in (0,) + NEAR_FIRST:
            self.across(step).wait_recv()
        for source in range(RING):
            self.result[1 - core, source] = self.other_half[
                lax.rem(at_partner - source + RING, RING)
            ].astype(jnp.float32)

    def drain(self):
        self.swap().wait_send()
        for step in range(RING):
            self.across(step).wait_send()

        def one(step, carry):
            self.wide_copy(step).wait_send()
            self.middle_copy(step).wait_send()
            self.last_copy(step).wait_send()
            self.chunk_copy(step).wait_send()
            return carry

        lax.fori_loop(1, RING, one, 0)


def reduce_scratch(rows, lanes):
    low, high = jnp.bfloat16, jnp.float32
    kinds = [low, low, high, low, low, low, low, low, low]
    return [pltpu.VMEM((2, RING, rows, lanes), kind) for kind in kinds] + [
        pltpu.SemaphoreType.DMA((2, 1 + RING)),
        pltpu.SemaphoreType.DMA((2, 1 + RING)),
        pltpu.SemaphoreType.DMA((2, 4, RING)),
        pltpu.SemaphoreType.DMA((2, 4, RING)),
    ]


def gelu_parts(pre):
    square = pre * pre
    bent = jnp.tanh(GELU_SLOPE * pre * (1.0 + GELU_CUBIC * square))
    value = 0.5 * pre * (1.0 + bent)
    slope = 0.5 * (1.0 + bent) + 0.5 * pre * (1.0 - bent * bent) * GELU_SLOPE * (
        1.0 + 3.0 * GELU_CUBIC * square
    )
    return value, slope


def halo_devices():
    lat = lax.axis_index("lat")
    lon = lax.axis_index("lon")
    lats = lax.axis_size("lat")
    lons = lax.axis_size("lon")
    at_top = lax.div(lats - 1 - lat, lats - 1)
    at_bottom = lax.div(lat, lats - 1)
    right = lax.rem(lon + 1, lons)
    left = lax.rem(lon + lons - 1, lons)
    ends = []
    for at_end, step, row_slot in ((at_top, -1, 1 - at_top), (at_bottom, 1, at_bottom)):
        far_lat = lat + step * (1 - at_end)
        turn = at_end * (lons // 2)
        ends.append(
            (
                row_slot,
                (far_lat, lax.rem(lon + turn, lons)),
                (far_lat, lax.rem(right + turn, lons)),
                (far_lat, lax.rem(left + turn, lons)),
            )
        )
    return (lat, right), (lat, left), ends


def greet_halo(barrier):
    right, left, ends = halo_devices()
    others = [right, left]
    for _, straight, to_right, to_left in ends:
        others += [straight, to_right, to_left]
    for other in others:
        pl.semaphore_signal(barrier, inc=1, device_id=other, device_id_type=MESH)
    return len(others)


def halo_outgoing(stage, halo):
    own, first_cols, last_cols, west, east, row_in, send_sem, recv_sem = halo
    rows = own.shape[1]
    right, left, ends = halo_devices()
    count = 0

    def copy(source, target, slot, device):
        nonlocal count
        count += 1
        return pltpu.make_async_remote_copy(
            src_ref=source, dst_ref=target, send_sem=send_sem.at[stage, count - 1],
            recv_sem=recv_sem.at[stage, slot], device_id=device, device_id_type=MESH,
        )

    outgoing = []
    for (slot, straight, to_right, to_left), row in zip(ends, (0, rows - 1)):
        edge = slot * (rows + 1)
        outgoing += [
            copy(last_cols.at[stage, row], west.at[stage, edge], 4 + slot, to_right),
            copy(first_cols.at[stage, row], east.at[stage, edge], 6 + slot, to_left),
            copy(own.at[stage, row], row_in.at[stage, slot], 2 + slot, straight),
        ]
    inner = pl.ds(1, rows)
    outgoing += [
        copy(last_cols.at[stage], west.at[stage, inner], 0, right),
        copy(first_cols.at[stage], east.at[stage, inner], 1, left),
    ]
    return outgoing


def halo_incoming(stage, halo):
    own, first_cols, last_cols, west, east, row_in, send_sem, recv_sem = halo
    rows = own.shape[1]
    right, left, _ = halo_devices()

    def copy(source, target, slot, device):
        return pltpu.make_async_remote_copy(
            src_ref=source, dst_ref=target, send_sem=send_sem.at[stage, slot],
            recv_sem=recv_sem.at[stage, slot], device_id=device, device_id_type=MESH,
        )

    inner = pl.ds(1, rows)
    incoming = [
        copy(last_cols.at[stage], west.at[stage, inner], 0, right),
        copy(first_cols.at[stage], east.at[stage, inner], 1, left),
    ]
    for slot in range(2):
        edge = slot * (rows + 1)
        incoming += [
            copy(own.at[stage, 0], row_in.at[stage, slot], 2 + slot, right),
            copy(last_cols.at[stage, 0], west.at[stage, edge], 4 + slot, right),
            copy(first_cols.at[stage, 0], east.at[stage, edge], 6 + slot, right),
        ]
    return incoming


def halo_prepare(stage, field, halo):
    own, first_cols, last_cols = halo[:3]
    own[stage] = field.astype(own.dtype)
    first_cols[stage] = field[:, :RIM].astype(own.dtype)
    last_cols[stage] = field[:, -RIM:].astype(own.dtype)


def halo_send(stage, halo):
    for copy in halo_outgoing(stage, halo):
        copy.start()


def halo_receive(stage, halo, extended):
    own, _, _, west, east, row_in = halo[:6]
    rows, cols = own.shape[1], own.shape[2]
    period = cols + 2 * RIM

    for row in range(rows):
        start = (row + 1) * period + 2 * RIM
        extended[start : start + cols] = own[stage, row]
    for copy in halo_incoming(stage, halo):
        copy.wait_recv()
    for slot in range(2):
        start = slot * (rows + 1) * period + 2 * RIM
        extended[start : start + cols] = row_in[stage, slot]
    west_rim = west[stage].astype(jnp.float32)
    east_rim = east[stage].astype(jnp.float32)
    blank = jnp.zeros((1, RIM, LANES), jnp.float32)
    rims = jnp.concatenate(
        [
            jnp.concatenate([blank, east_rim], axis=0),
            jnp.concatenate([west_rim, blank], axis=0),
        ],
        axis=1,
    ).astype(own.dtype)
    for row in range(rows + 3):
        extended[row * period : row * period + 2 * RIM] = rims[row]


def apply_bands(bands, extended, spread):
    rows = bands.shape[0]
    kernels = spread.shape[1] // LANES
    cols = spread.shape[0] // rows
    period = cols + 2 * RIM
    group = 4

    def some_rows(index, carry):
        for part in range(group):
            row = index * group + part
            window = extended[pl.ds(pl.multiple_of(row * period, period), LANES)]
            made = jnp.dot(
                bands[row], window, preferred_element_type=jnp.float32
            ).astype(spread.dtype)
            for kernel in range(kernels):
                spread[
                    pl.ds(pl.multiple_of(row * cols, cols), cols),
                    kernel * LANES : (kernel + 1) * LANES,
                ] = made[kernel * cols : (kernel + 1) * cols]
        return carry

    lax.fori_loop(0, rows // group, some_rows, 0)


def slant(lined, cols):
    kernels = lined.shape[0]
    level = jnp.broadcast_to(lined[:, None, :], (kernels, cols, LANES))
    return pltpu.roll(level, 0, 2, stride=1, stride_axis=1).reshape(kernels * cols, LANES)


def shifted_lane(shape):
    return lax.broadcasted_iota(jnp.int32, shape, 1) + (PERIOD - LEAD)


def within(lane, width):
    return jnp.abs((lane & (PERIOD - 1)) - RIM // 2) <= width


def fill_ahead(table, widths, bands, first, cols):
    def one_row(row, carry):
        seen = table[first + row][:, :LANES]
        seen = jnp.where(within(shifted_lane(seen.shape), widths[first + row]), seen, 0.0)
        bands[row] = slant(seen, cols).astype(bands.dtype)
        return carry

    lax.fori_loop(0, bands.shape[0], one_row, 0)


def fill_back(table, widths, bands, first, cols):
    last_row = table.shape[0] - 1

    def one_row(row, carry):
        total = None
        for side in range(3):
            at = jnp.minimum(jnp.maximum(first + row + side - 1, 0), last_row)
            seen = table[at][:, LANES:]
            if side != 1:
                end = 0 if side == 0 else last_row
                seen = jnp.where(first + row == end, pltpu.roll(seen, LANES // 2, 1), seen)
            lane = shifted_lane(seen.shape)
            wanted = within(lane, widths[at]) & (lane // PERIOD == side + 1)
            seen = jnp.where(wanted, seen, 0.0)
            total = seen if total is None else total + seen
        bands[row] = slant(total, cols).astype(bands.dtype)
        return carry

    lax.fori_loop(0, bands.shape[0], one_row, 0)


def mixed_back(spread, weight):
    total = None
    for kernel in range(weight.shape[0]):
        term = lax.dot_general(
            spread[:, kernel * LANES : (kernel + 1) * LANES],
            weight[kernel],
            (((1,), (1,)), ((), ())),
            preferred_element_type=jnp.float32,
        )
        total = term if total is None else total + term
    return total


def whole_kernel(
    fields, cotangent, weight_one, weight_two, table, widths,
    output, dfields, grad_one, grad_two,
    bands_ahead, bands_back, extended, u_one, u_two, v_vals, slope_one, dhidden, terms,
    own, first_cols, last_cols, west, east, row_in, halo_send_sem, halo_recv_sem, *scratch
):
    rows, cols, channels = fields.shape
    flat = (rows * cols, channels)
    halo = (own, first_cols, last_cols, west, east, row_in, halo_send_sem, halo_recv_sem)
    here = coordinates()
    chain_one = Chain(0, here, terms, grad_one, scratch)
    chain_two = Chain(1, here, terms, grad_two, scratch)
    barrier = pltpu.get_barrier_semaphore()
    awaited = greet_halo(barrier) + greet_reducers(here, barrier)

    halo_prepare(0, fields[...].astype(jnp.float32), halo)
    extended[...] = jnp.zeros(extended.shape, extended.dtype)
    first = lax.axis_index("lat") * rows
    fill_ahead(table, widths, bands_ahead, first, cols)
    pl.semaphore_wait(barrier, awaited)
    halo_send(0, halo)
    fill_back(table, widths, bands_back, first, cols)
    halo_receive(0, halo, extended)

    apply_bands(bands_ahead, extended, u_one)
    mix_one = weight_one[...].reshape(-1, channels)
    pre = jnp.dot(u_one[...], mix_one, preferred_element_type=jnp.float32)
    value, slope = gelu_parts(pre)
    slope_one[...] = slope
    hidden = fields[...].astype(jnp.float32) + value.reshape(rows, cols, channels)
    halo_prepare(1, hidden, halo)
    halo_send(1, halo)
    halo_receive(1, halo, extended)

    apply_bands(bands_ahead, extended, u_two)
    mix_two = weight_two[...].reshape(-1, channels)
    pre = jnp.dot(u_two[...], mix_two, preferred_element_type=jnp.float32)
    value, slope = gelu_parts(pre)
    upstream = cotangent[...].astype(jnp.float32)
    dconv = upstream * slope.reshape(rows, cols, channels)
    halo_prepare(2, dconv, halo)
    halo_send(2, halo)
    output[...] = (
        own[1].astype(jnp.float32) + value.reshape(rows, cols, channels)
    ).astype(output.dtype)
    terms[1] = lax.dot_general(
        u_two[...], own[2].reshape(flat), (((0,), (0,)), ((), ())),
        preferred_element_type=jnp.float32,
    ).reshape(terms.shape[1:])
    chain_two.begin()
    halo_receive(2, halo, extended)
    chain_two.scatter()

    apply_bands(bands_back, extended, v_vals)
    arrived = upstream.reshape(flat) + mixed_back(v_vals, weight_two)
    dhidden[...] = arrived
    dconv = (arrived * slope_one[...]).reshape(rows, cols, channels)
    own[3] = dconv.astype(own.dtype)
    terms[0] = lax.dot_general(
        u_one[...], own[3].reshape(flat), (((0,), (0,)), ((), ())),
        preferred_element_type=jnp.float32,
    ).reshape(terms.shape[1:])
    chain_one.begin()
    halo_prepare(3, dconv, halo)
    halo_send(3, halo)
    chain_two.sum_first()
    chain_one.scatter()
    chain_two.sum_second()

    halo_receive(3, halo, extended)
    apply_bands(bands_back, extended, v_vals)
    total = dhidden[...] + mixed_back(v_vals, weight_one)
    dfields[...] = total.reshape(rows, cols, channels).astype(dfields.dtype)

    chain_one.sum_first()
    chain_two.sum_third()
    chain_one.sum_second()
    chain_two.gather()
    chain_one.sum_third()
    chain_two.drain()
    chain_one.gather()
    chain_one.drain()
    for stage in range(own.shape[0]):
        for copy in halo_outgoing(stage, halo):
            copy.wait_send()


def tap_table(basis_raw):
    _, _, row_taps, lon_taps = basis_raw.shape
    shape = (row_taps, lon_taps, 2 * LANES)
    row_tap, lon_tap, lane = (lax.broadcasted_iota(jnp.int32, shape, dim) for dim in range(3))
    ahead = LEAD + PERIOD * row_tap + lon_tap
    back = LANES + LEAD + PERIOD * (row_taps - 1 - row_tap) + lon_taps - 1 - lon_tap
    placed = ((lane == ahead) | (lane == back)).astype(basis_raw.dtype)
    return jnp.einsum("kirt,rtp->ikp", basis_raw, placed, preferred_element_type=jnp.float32)


def body(fields, weight_one, weight_two, basis_raw, widths, cotangent):
    rows, cols, channels = fields.shape
    kernels = weight_one.shape[0]
    scale = 1.0 / math.sqrt(rows * lax.axis_size("lat") * cols * lax.axis_size("lon"))
    grad_rows = kernels * channels // (2 * RING)
    low, high = jnp.bfloat16, jnp.float32
    height = (rows + 3) * (cols + 2 * RIM)
    stages = 4
    scratch = [
        pltpu.VMEM((rows, kernels * cols, LANES), low),
        pltpu.VMEM((rows, kernels * cols, LANES), low),
        pltpu.VMEM((height, channels), low),
        pltpu.VMEM((rows * cols, kernels * channels), low),
        pltpu.VMEM((rows * cols, kernels * channels), low),
        pltpu.VMEM((rows * cols, kernels * channels), low),
        pltpu.VMEM((rows * cols, channels), high),
        pltpu.VMEM((rows * cols, channels), high),
        pltpu.VMEM((2, 2, RING, grad_rows, channels), high),
        pltpu.VMEM((stages, rows, cols, channels), low),
        pltpu.VMEM((stages, rows, RIM, channels), low),
        pltpu.VMEM((stages, rows, RIM, channels), low),
        pltpu.VMEM((stages, rows + 2, RIM, channels), low),
        pltpu.VMEM((stages, rows + 2, RIM, channels), low),
        pltpu.VMEM((stages, 2, cols, channels), low),
        pltpu.SemaphoreType.DMA((stages, 8)),
        pltpu.SemaphoreType.DMA((stages, 8)),
    ] + reduce_scratch(grad_rows, channels)
    wide = jax.ShapeDtypeStruct((2, RING, grad_rows, channels), high)
    output, dfields, grad_one, grad_two = pl.pallas_call(
        whole_kernel,
        out_shape=(
            jax.ShapeDtypeStruct(fields.shape, low),
            jax.ShapeDtypeStruct(fields.shape, low),
            wide,
            wide,
        ),
        in_specs=[pl.BlockSpec(memory_space=pltpu.VMEM)] * 5
        + [pl.BlockSpec(memory_space=pltpu.SMEM)],
        out_specs=(pl.BlockSpec(memory_space=pltpu.VMEM),) * 4,
        scratch_shapes=scratch,
        compiler_params=pltpu.CompilerParams(collective_id=0, has_side_effects=True),
    )(fields, cotangent, weight_one, weight_two, tap_table(basis_raw), widths)
    shape = (kernels, channels, channels)
    return output, dfields, grad_one.reshape(shape) * scale, grad_two.reshape(shape) * scale


def solution(mesh):
    placed = (P("lat", "lon", None), P(), P(), P(), P(), P("lat", "lon", None))
    return jax.shard_map(
        body,
        mesh=mesh,
        in_specs=placed,
        out_specs=(P("lat", "lon", None), P("lat", "lon", None), P(), P()),
        check_vma=False,
    )
```
